256 devices in a mesh: patch: 32 (over z_hi, y, core), helper: 8 (over z_lo, x).
Axes of the slice: x: 4, y: 4, z: 8 (z_hi: 4, z_lo: 2; z = z_hi * 2 + z_lo), core: 2. Of those that a mesh axis runs over, the one named last changes fastest.
Arguments:
- dens: float32 [8192, 16, 128], P(('patch', 'helper')), may hold values from -6 to 6
- upsample: float32 [128, 16], replicated, may hold values from -1.5 to 1.5
- src_geom: float32 [12288, 7, 128], P('patch'), may hold values from -1 to 3, as said below
- targ: float32 [10, 131072], P(None, ('patch', 'helper')), may hold values from -1 to 3, as said below
- lists: int32 [1024, 16], P(('patch', 'helper')), may hold values from 0 to 383, as said below
- lens: int32 [1024], P(('patch', 'helper')), may hold values from 1 to 15, as said below
Outputs:
- near: float32 [131072, 128], P(('patch', 'helper'))
The draws below stay inside these ranges and needn't reach their ends.
Inputs may be any that keep to these rules, and one draw needn't show every extreme that they name: `src_geom`: points lie at heights -0.01 to 0 with positive weights and unit normals pointing upward by 0.3 or more. `targ`: targets lie at heights 0.07 to 0.1, normals are unit with a height component of 0.9 or more, tangents unit, with first component 0, and orthogonal to the normals, radii 0.02 to 0.03. `lists`: the 16 entries of a block are distinct. Indices below 64 name the previous group's last panels, the next 256 the group's own, the rest the next group's first panels; groups form a closed cycle. Slots from lens on are unused. `lens`: the lengths of the 32 blocks of one patch group sum to exactly 256.
All inputs are finite; a program needn't handle non-finite values.
Results may differ from the reference program's by a relative error of at most 0.0003.
Values sent between devices are 32-bit elements; how exact they have to be, the bound alone decides.
No kernel may reach another device: no remote copies, remote signals or barrier semaphores. Data moves between devices by JAX's collectives and lax.ppermute only.
A program may use at most 128 MiB of HBM per device.

```python
import math
import jax
import jax.numpy as jnp
from jax import lax

NODES = 16
UPS = 128
NRHS = 128
BLOCK = 128
CHECKS = 16
NLIST = 16
CB_DEV = 4
PG = 256
HW = 64
EXT = 384
PANELS = 8192
CB_GROUP = 32
CBLOCKS = 1024
N_PATCH = 32
N_HELPER = 8


columns_per_row = 16


cell_side = 0.0625


def group_plan(key):
    keys = jax.random.split(jax.random.fold_in(key, 23), 3)
    halfway = CB_GROUP // 2
    heavy = jax.random.randint(keys[0], (N_PATCH, halfway), NLIST - NLIST // 4, NLIST)
    heavy = heavy.at[:, 0].set(NLIST - 1)
    paired = jnp.concatenate([heavy, NLIST - heavy], axis=1)
    homes = jax.random.randint(keys[2], (N_PATCH, CB_GROUP), HW, HW + PG)
    homes = homes.at[:, 0].set(HW).at[:, 1].set(HW + PG - 1)
    ordering = jax.vmap(lambda subkey: jax.random.permutation(subkey, N_HELPER))(jax.random.split(keys[1], N_PATCH))

    def shuffle(values):
        arranged = values.reshape(N_PATCH, N_HELPER, CB_DEV)
        return jnp.take_along_axis(arranged, ordering[:, :, None], axis=1).reshape(N_PATCH * CB_GROUP).astype(jnp.int32)
    return (shuffle(paired), shuffle(homes))


def home_cells(key):
    lengths, homes = group_plan(key)
    return homes


def draw_src_geom(key, part):
    rowcount = EXT * N_PATCH
    keys = jax.random.split(jax.random.fold_in(key, 11), 4)
    cells = jnp.arange(rowcount, dtype=jnp.int32) % EXT
    corner = jnp.stack([cells % columns_per_row, cells // columns_per_row]).astype(jnp.float32)
    across = (jnp.transpose(corner)[:, :, None] + jax.random.uniform(keys[0], (rowcount, 2, UPS), jnp.float32)) * cell_side
    height = -0.01 * jax.random.uniform(keys[1], (rowcount, 1, UPS), jnp.float32)
    raw = jax.random.uniform(keys[2], (rowcount, 3, UPS), jnp.float32, -1.0, 1.0) + jnp.array([0.0, 0.0, 2.0], jnp.float32)[None, :, None]
    normal = raw / jnp.sqrt(jnp.sum(raw * raw, axis=1, keepdims=True))
    quad_weight = jnp.exp(jax.random.uniform(keys[3], (rowcount, 1, UPS), jnp.float32, math.log(0.001), math.log(0.01)))
    return jnp.concatenate([across, height, normal, quad_weight], axis=1)


def draw_targ(key, part):
    number = CBLOCKS * BLOCK
    keys = jax.random.split(jax.random.fold_in(key, 17), 4)
    homes = jnp.repeat(home_cells(key), BLOCK, total_repeat_length=number)
    corner = jnp.stack([homes % columns_per_row, homes // columns_per_row]).astype(jnp.float32)
    across = (corner + jax.random.uniform(keys[0], (2, number), jnp.float32)) * cell_side
    height = 0.07 + 0.03 * jax.random.uniform(keys[1], (1, number), jnp.float32)
    raw = jax.random.uniform(keys[2], (3, number), jnp.float32, -1.0, 1.0) + jnp.array([0.0, 0.0, 4.0], jnp.float32)[:, None]
    normal = raw / jnp.sqrt(jnp.sum(raw * raw, axis=0, keepdims=True))
    sideways = jnp.stack([jnp.zeros_like(normal[2]), normal[2], -normal[1]])
    tangent = sideways / jnp.sqrt(jnp.sum(sideways * sideways, axis=0, keepdims=True))
    radius = 0.02 + 0.01 * jax.random.uniform(keys[3], (1, number), jnp.float32)
    return jnp.concatenate([across, height, normal, tangent, radius], axis=0)


def draw_lists(key, part):
    homes = home_cells(key)
    cells = jnp.arange(EXT, dtype=jnp.int32)
    column_gap = cells[None, :] % columns_per_row - (homes % columns_per_row)[:, None]
    row_gap = cells[None, :] // columns_per_row - (homes // columns_per_row)[:, None]
    distance = column_gap * column_gap + row_gap * row_gap
    own_cell = ((cells >= HW) & (cells < HW + PG)).astype(jnp.int32)
    jitter = jax.random.randint(jax.random.fold_in(key, 31), (CBLOCKS, EXT), 1, 257) * own_cell[None, :]
    scores = (distance * 257 + jitter) * EXT + cells[None, :]
    ordering = jnp.argsort(scores, axis=1)
    return ordering[:, :NLIST].astype(jnp.int32)


def draw_lens(key, part):
    lengths, homes = group_plan(key)
    return lengths


def levels(own_key, extent, cuts, low, largest):
    def one(axis_at, parts):
        steps = jax.random.uniform(jax.random.fold_in(jax.random.fold_in(own_key, 6), axis_at), (parts,), jnp.float32, low / len(cuts), largest / len(cuts))
        return jnp.repeat(jnp.exp(steps), extent[axis_at] // parts).reshape((-1,) + (1,) * (len(extent) - axis_at - 1))

    gain = one(*cuts[0])
    for cut in cuts[1:]:
        gain = gain * one(*cut)
    return gain


def normal_values(key, dims, spread, reach, cuts=(), kind=jnp.bfloat16):
    factor_of = levels(key, dims, cuts, -0.22, 0.18) if cuts else 1.0
    entries = jax.random.normal(key, dims, jnp.float32) * spread * factor_of
    return jnp.minimum(jnp.maximum(entries, -reach), reach).astype(kind)


def setup_inputs(seed: int = 0) -> dict:
    streams_of = jax.random.split(jax.random.key(seed), 7)
    return {
        "dens": normal_values(streams_of[0], (PANELS, NODES, NRHS), 1.0, 6.0, ((0, 256),), jnp.float32),
        "upsample": normal_values(streams_of[1], (UPS, NODES), NODES ** -0.5, 1.5, (), jnp.float32),
        "src_geom": draw_src_geom(jax.random.fold_in(streams_of[6], 71), 0),
        "targ": draw_targ(jax.random.fold_in(streams_of[6], 71), 0),
        "lists": draw_lists(jax.random.fold_in(streams_of[6], 71), 0),
        "lens": draw_lens(jax.random.fold_in(streams_of[6], 71), 0),
    }


screening = 2.0
coupling = 1.0
check_group = 4
highest = lax.Precision.HIGHEST

def circle_weights(samples):
    angles = 2.0 * math.pi * jnp.arange(samples, dtype=jnp.float32) / samples
    return 0.75 / (samples * (1.25 + jnp.cos(angles)))

def check_points(target_block, samples):
    angles = 2.0 * math.pi * jnp.arange(samples, dtype=jnp.float32) / samples
    position = target_block[0:3]
    normal = target_block[3:6]
    tangent = target_block[6:9]
    radius = target_block[9]
    center = position + radius[None, :] * normal
    spokes = jnp.cos(angles)[None, :, None] * normal[:, None, :] + jnp.sin(angles)[None, :, None] * tangent[:, None, :]
    return center[:, None, :] + 2.0 * radius[None, None, :] * spokes

def kernel_part(points, weights, sources):
    across = [points[axis_id][:, :, None] - sources[axis_id][None, None, :] for axis_id in range(3)]
    square = across[0] * across[0] + across[1] * across[1] + across[2] * across[2]
    spacing = jnp.sqrt(square)
    falloff = jnp.exp(-screening * spacing) / (4.0 * math.pi * spacing)
    facing = across[0] * sources[3] + across[1] * sources[4] + across[2] * sources[5]
    kernel_value = falloff * (coupling + facing * (1.0 + screening * spacing) / square)
    return lax.optimization_barrier(jnp.sum(weights[:, None, None] * kernel_value, axis=0))

def folded_kernel(target_block, sources):
    points = check_points(target_block, CHECKS)
    weights = circle_weights(CHECKS)
    rounds = CHECKS // check_group
    stacked_points = points.reshape(3, rounds, check_group, points.shape[2]).transpose(1, 0, 2, 3)
    stacked_weights = weights.reshape(rounds, check_group)

    def add_round(running, payload):
        return (running + kernel_part(payload[0], payload[1], sources), None)
    initial = jnp.zeros((points.shape[2], sources.shape[1]), jnp.float32)
    running, ignored = lax.scan(add_round, initial, (stacked_points, stacked_weights))
    return running

def upsample_panels(upsample, node_values):
    return jnp.einsum('jq,eqr->ejr', upsample, node_values, precision=highest, preferred_element_type=jnp.float32)

def block_value(target_block, listed, length, geometry, charges):
    chosen = jnp.take(geometry, listed, axis=0)
    sources = jnp.transpose(chosen, (1, 0, 2)).reshape(chosen.shape[1], -1)
    live = (jnp.arange(listed.shape[0], dtype=jnp.int32) < length).astype(jnp.float32)
    loads = (jnp.take(charges, listed, axis=0) * live[:, None, None]).reshape(-1, charges.shape[2])
    kernel = folded_kernel(target_block, sources)
    return jnp.dot(kernel, loads, precision=highest, preferred_element_type=jnp.float32)

def reference(dens, upsample, src_geom, targ, lists, lens):
    groups = N_PATCH
    node_values = dens.reshape(groups, PG, NODES, NRHS)
    previous = jnp.roll(node_values, 1, axis=0)[:, PG - HW:]
    following = jnp.roll(node_values, -1, axis=0)[:, :HW]
    extended = jnp.concatenate([previous, node_values, following], axis=1)
    geometry = src_geom.reshape(groups, EXT, 7, UPS)
    targets = targ.reshape(10, groups, CB_GROUP, BLOCK).transpose(1, 2, 0, 3)
    listed = lists.reshape(groups, CB_GROUP, NLIST)
    lengths = lens.reshape(groups, CB_GROUP)

    def one_group(payload):
        wide_nodes, geom_group, targ_group, list_group, length_group = payload
        charges = upsample_panels(upsample, wide_nodes) * geom_group[:, 6, :, None]
        return lax.map(lambda element: block_value(element[0], element[1], element[2], geom_group, charges), (targ_group, list_group, length_group))
    potentials = lax.map(one_group, (extended, geometry, targets, listed, lengths))
    return potentials.reshape(groups * CB_GROUP * BLOCK, NRHS)
```

```python
import functools
import math

import jax
import jax.numpy as jnp
from jax import lax
from jax.experimental import pallas as pl
from jax.experimental.pallas import tpu as pltpu
from jax.sharding import PartitionSpec as P

CHECKS = 16
NODES = 16
LANES = 128
F32 = jnp.float32
BF16 = jnp.bfloat16

LN2 = math.log(2.0)
KAPPA = 2.0 / LN2
REACH = 0.5

LEFT = (0, 0, 1, 1, 0, 2)
RIGHT = (0, 1, 0, 1, 2, 0)
DEPTH = 64
RING = 16
AHEAD = 8
VMEM_KEPT = 67043328 - 2500000


def angle(m):
    return 2.0 * math.pi * m / CHECKS


def log_weight(m):
    weight = 0.75 / (CHECKS * (1.25 + math.cos(angle(m))))
    return math.log2(weight * KAPPA / (4.0 * math.pi))


def halves(x):
    high = x.astype(BF16)
    return high, (x - high.astype(F32)).astype(BF16)


def thirds(x):
    high = x.astype(BF16).astype(F32)
    rest = x - high
    middle = rest.astype(BF16).astype(F32)
    return high, middle, rest - middle


def stacked(features, order):
    parts = thirds(features)
    rows = [parts[i] for i in order]
    rows.append(jnp.zeros((DEPTH - 8 * len(order), LANES), F32))
    return jnp.concatenate(rows, axis=0)


def total_of(x):
    return jnp.sum(x, axis=0, keepdims=True)


def coefficients_body(lists, lens, targ, ups, geom, out, src, wts, lhs, tile, pairs, org, far, table, sem, *, first, count):
    zero = jnp.zeros((1, LANES), F32)
    one = jnp.ones((1, LANES), F32)

    def block_rows(b, at):
        def row(l, at):
            table[0, at] = b
            table[1, at] = l
            return at + 1

        return lax.fori_loop(0, lens[first + b], row, at)

    items = lax.fori_loop(0, count, block_rows, jnp.int32(0))

    def item(i):
        i = jnp.minimum(i, items - 1)
        return table[0, i], table[1, i]

    def fetch(i):
        b, l = item(i)
        slot = i & (RING - 1)
        return pltpu.make_async_copy(geom.at[:, lists[first + b, l]], src.at[slot, pl.ds(0, 7)], sem.at[slot])

    for i in range(AHEAD):
        fetch(jnp.int32(i)).start()
    far[...] = jnp.zeros_like(far)

    def circle(b):
        t = targ[:, pl.ds(pl.multiple_of((first + b) * LANES, LANES), LANES)]
        radius = t[9:10] * KAPPA
        return t[0:3] * KAPPA, radius * t[3:6], 2 * radius * t[3:6], 2 * radius * t[6:9]

    def build(b, carry):
        position, lift, normal, tangent = circle(b)
        origin = jnp.broadcast_to(jnp.mean(position, axis=1, keepdims=True), (3, LANES))
        org[b, 0:3] = origin
        center = position - origin + lift
        for m in range(CHECKS):
            point = center + math.cos(angle(m)) * normal + math.sin(angle(m)) * tangent
            square = total_of(point * point)
            far[0:1] = jnp.maximum(far[0:1], square)
            features = jnp.concatenate([square, point, one, zero, zero, zero], axis=0)
            wts[b, :, m * LANES : (m + 1) * LANES] = stacked(features, LEFT).astype(BF16)
        return carry

    lax.fori_loop(0, count, build, 0)
    out[...] = jnp.zeros_like(out)

    def prepare(i, slot):
        b, _ = item(i)
        g = src[i & (RING - 1), 0:7]
        y = g[0:3] * KAPPA - org[b, 0:3]
        n = g[3:6] * KAPPA
        square = total_of(y * y)
        far[1:2] = jnp.maximum(far[1:2], square)
        for_square = jnp.concatenate([one, -2.0 * y, square, zero, zero, zero], axis=0)
        for_facing = jnp.concatenate([zero, n, -total_of(n * y), zero, zero, zero], axis=0)
        both = jnp.concatenate([stacked(for_square, RIGHT), stacked(for_facing, RIGHT)], axis=0)
        both = both.T.astype(BF16)
        for j in range(8):
            lhs[slot, 32 * j : 32 * j + 16] = both[16 * j : 16 * j + 16, 0:DEPTH]
            lhs[slot, 32 * j + 16 : 32 * j + 32] = both[16 * j : 16 * j + 16, DEPTH : 2 * DEPTH]

    def two_points(b, slot, k):
        return jnp.dot(lhs[slot], wts[b, :, 256 * k : 256 * k + 256], preferred_element_type=F32)

    def flush(i, g):
        b, l = item(i)
        high, low = halves(ups[...] * g[6:7])
        tile_high, tile_low = halves(tile[...])
        left = jnp.concatenate(
            [
                jnp.concatenate([high, high], axis=1),
                jnp.concatenate([low, jnp.zeros_like(low)], axis=1),
            ],
            axis=0,
        )
        right = jnp.concatenate([tile_high, tile_low], axis=0)
        sums = jnp.dot(left, right, preferred_element_type=F32)
        rows = pl.ds(pl.multiple_of(l * NODES, NODES), NODES)
        out[b, rows] = sums[0:NODES] + sums[NODES : 2 * NODES]

    def potential(square, facing, m):
        inverse = lax.rsqrt(square)
        single = jnp.exp2(log_weight(m) - square * inverse) * inverse
        return single + single * (inverse * (inverse + LN2) * facing)

    def step(i, carry):
        slot = i & 1
        fetch(i + 2).wait()
        fetch(i + AHEAD).start()
        last = jnp.maximum(i - 1, 0)
        flush(last, src[last & (RING - 1), 0:7])
        next_b, _ = item(i + 1)
        sums = [None] * 8
        for k in range(CHECKS // 2):
            r = pairs[:, 256 * k : 256 * k + 256]
            for half in range(2):
                cols = slice(LANES * half, LANES * half + LANES)
                for x in range(8):
                    value = potential(r[32 * x : 32 * x + 16, cols], r[32 * x + 16 : 32 * x + 32, cols], 2 * k + half)
                    sums[x] = value if sums[x] is None else sums[x] + value
            pairs[:, 256 * k : 256 * k + 256] = two_points(next_b, 1 - slot, k)
        for x in range(8):
            tile[16 * x : 16 * x + 16] = sums[x]
        prepare(i + 2, slot)
        return carry

    tile[...] = jnp.zeros_like(tile)
    for i in range(2):
        fetch(jnp.int32(i)).wait()
        prepare(jnp.int32(i), i)
    start_b, _ = item(jnp.int32(0))
    for k in range(CHECKS // 2):
        pairs[:, 256 * k : 256 * k + 256] = two_points(start_b, 0, k)
    lax.fori_loop(0, items, step, 0)
    flush(items - 1, src[(items - 1) & (RING - 1), 0:7])
    for i in range(2, AHEAD):
        fetch(items + i).wait()

    @pl.when(jnp.max(far[...]) > REACH * KAPPA * KAPPA)
    def _():
        def slow(i, carry):
            copy = fetch(i)
            copy.start()
            copy.wait()
            g = src[i & (RING - 1), 0:7]
            columns = jnp.concatenate([g, zero], axis=0).T
            y = [columns[:, a : a + 1] * KAPPA for a in range(3)]
            n = [columns[:, a + 3 : a + 4] * KAPPA for a in range(3)]
            position, lift, normal, tangent = circle(item(i)[0])
            center = position + lift
            tile[...] = jnp.zeros_like(tile)
            for m in range(CHECKS):
                point = center + math.cos(angle(m)) * normal + math.sin(angle(m)) * tangent
                for x in range(8):
                    rows = slice(16 * x, 16 * x + 16)
                    d = [point[a : a + 1] - y[a][rows] for a in range(3)]
                    square = d[0] * d[0] + d[1] * d[1] + d[2] * d[2]
                    facing = d[0] * n[0][rows] + d[1] * n[1][rows] + d[2] * n[2][rows]
                    tile[rows] += potential(square, facing, m)
            flush(i, g)
            return carry

        lax.fori_loop(0, items, slow, 0)


def coefficients(lists, lens, targ, ups, geom, first, count):
    pairs = 15 * count
    return pl.pallas_call(
        functools.partial(coefficients_body, first=first, count=count),
        grid_spec=pltpu.PrefetchScalarGridSpec(
            num_scalar_prefetch=2,
            grid=(1,),
            in_specs=[
                pl.BlockSpec(memory_space=pltpu.VMEM),
                pl.BlockSpec(memory_space=pltpu.VMEM),
                pl.BlockSpec(memory_space=pltpu.HBM),
            ],
            out_specs=pl.BlockSpec(memory_space=pltpu.VMEM),
            scratch_shapes=[
                pltpu.VMEM((RING, 8, LANES), F32),
                pltpu.VMEM((count, DEPTH, CHECKS * LANES), BF16),
                pltpu.VMEM((2, 2 * LANES, DEPTH), BF16),
                pltpu.VMEM((LANES, LANES), F32),
                pltpu.VMEM((2 * LANES, CHECKS * LANES), F32),
                pltpu.VMEM((count, 8, LANES), F32),
                pltpu.VMEM((8, LANES), F32),
                pltpu.SMEM((2, 16 * count), jnp.int32),
                pltpu.SemaphoreType.DMA((RING,)),
            ],
        ),
        out_shape=jax.ShapeDtypeStruct((count, 16 * NODES, LANES), F32),
        cost_estimate=pl.CostEstimate(
            flops=pairs * 128 * 128 * 16 * 40, bytes_accessed=2 << 20, transcendentals=pairs * 128 * 128 * 32
        ),
        compiler_params=pltpu.CompilerParams(vmem_limit_bytes=VMEM_KEPT),
        name="coefficients%d" % first,
    )(lists, lens, targ, ups, geom)


def combine_body(lists, place, *refs, parts):
    coefs = refs[:parts]
    shards = refs[parts : parts + 8]
    edges = refs[parts + 8 : parts + 16]
    out, wide, sem = refs[parts + 16 :]
    me = place[0]

    def owner(k):
        return (me + 8 - k) & 7

    def copies(k):
        o = owner(k)
        own = pltpu.make_async_copy(shards[k], wide.at[pl.ds(64 + 32 * o, 32)], sem.at[k])
        row = jnp.where(o >= 6, 32 * (o - 6), 320 + 32 * o)
        edge = pltpu.make_async_copy(edges[k], wide.at[pl.ds(row, 32)], sem.at[8 + k])
        return own, edge, (o >= 6) | (o < 2)

    for k in range(8):
        own, edge, used = copies(k)
        own.start()
        pl.when(used)(edge.start)
    for k in range(8):
        own, edge, used = copies(k)
        own.wait()
        pl.when(used)(edge.wait)
    per = 4 // parts
    for b in range(4):
        nodes = jnp.concatenate([wide[lists[b, l]] for l in range(16)], axis=0)
        high, low = halves(nodes)
        c = coefs[b // per][b % per].T
        c_high, c_low = halves(c)
        value = jnp.dot(c_high, high, preferred_element_type=F32)
        value += jnp.dot(c_high, low, preferred_element_type=F32)
        value += jnp.dot(c_low, high, preferred_element_type=F32)
        out[b * LANES : (b + 1) * LANES] = value


def combine(lists, place, coefs, shards, edges):
    parts = len(coefs)
    return pl.pallas_call(
        functools.partial(combine_body, parts=parts),
        grid_spec=pltpu.PrefetchScalarGridSpec(
            num_scalar_prefetch=2,
            grid=(1,),
            in_specs=[pl.BlockSpec(memory_space=pltpu.VMEM)] * parts + [pl.BlockSpec(memory_space=pl.ANY)] * 16,
            out_specs=pl.BlockSpec(memory_space=pltpu.VMEM),
            scratch_shapes=[
                pltpu.VMEM((384, NODES, LANES), F32),
                pltpu.SemaphoreType.DMA((16,)),
            ],
        ),
        out_shape=jax.ShapeDtypeStruct((4 * LANES, LANES), F32),
        cost_estimate=pl.CostEstimate(flops=4 << 24, bytes_accessed=4 << 20, transcendentals=0),
        compiler_params=pltpu.CompilerParams(vmem_limit_bytes=24 << 20),
        name="combine",
    )(lists, place, *coefs, *shards, *edges)


def on_device(dens, upsample, src_geom, targ, lists, lens):
    groups = lax.axis_size("patch")
    both = ("patch", "helper")

    def at(g, h):
        return (g % groups) * 8 + h % 8

    shards = [dens]
    for k in range(1, 8):
        shards.append(lax.ppermute(dens, "helper", [(h, (h + k) % 8) for h in range(8)]))
    ups = upsample.T
    geom = jnp.transpose(src_geom, (1, 0, 2))
    coefs = [coefficients(lists, lens, targ, ups, geom, 0, 2)]
    *shards, coefs[0] = lax.optimization_barrier((*shards, coefs[0]))
    edges = []
    for k in range(8):
        moves = []
        for g in range(groups):
            moves += [(at(g, o + k), at(g + 1, o + k)) for o in (6, 7)]
            moves += [(at(g, o + k), at(g - 1, o + k)) for o in (0, 1)]
        edges.append(lax.ppermute(shards[k], both, moves))
    coefs.append(coefficients(lists, lens, targ, ups, geom, 2, 2))
    place = lax.axis_index("helper").astype(jnp.int32).reshape(1)
    return combine(lists, place, coefs, shards, edges)


def solution(mesh):
    in_specs = (
        P(("patch", "helper"), None, None),
        P(),
        P("patch", None, None),
        P(None, ("patch", "helper")),
        P(("patch", "helper"), None),
        P(("patch", "helper")),
    )
    out_specs = P(("patch", "helper"), None)
    return jax.shard_map(on_device, mesh=mesh, in_specs=in_specs, out_specs=out_specs, check_vma=False)
```

```python
import functools
import math

import jax
import jax.numpy as jnp
from jax import lax
from jax.experimental import pallas as pl
from jax.experimental.pallas import tpu as pltpu
from jax.sharding import PartitionSpec as P

CHECKS = 16
NODES = 16
LANES = 128
F32 = jnp.float32
BF16 = jnp.bfloat16

LN2 = math.log(2.0)
KAPPA = 2.0 / LN2
REACH = 0.5

LEFT = (0, 0, 1, 1, 0, 2)
RIGHT = (0, 1, 0, 1, 2, 0)
DEPTH = 64
RING = 16
AHEAD = 8
VMEM_KEPT = 67043328 - 3800000


def angle(m):
    return 2.0 * math.pi * m / CHECKS


def log_weight(m):
    weight = 0.75 / (CHECKS * (1.25 + math.cos(angle(m))))
    return math.log2(weight * KAPPA / (4.0 * math.pi))


def halves(x):
    high = x.astype(BF16)
    return high, (x - high.astype(F32)).astype(BF16)


def thirds(x):
    high = x.astype(BF16).astype(F32)
    rest = x - high
    middle = rest.astype(BF16).astype(F32)
    return high, middle, rest - middle


def stacked(features, order):
    parts = thirds(features)
    rows = [parts[i] for i in order]
    rows.append(jnp.zeros((DEPTH - 8 * len(order), LANES), F32))
    return jnp.concatenate(rows, axis=0)


def total_of(x):
    return jnp.sum(x, axis=0, keepdims=True)


def coefficients_body(lists, lens, targ, ups, geom, out, src, wts, lhs, tile, pairs, org, far, table, sem, *, first, count):
    zero = jnp.zeros((1, LANES), F32)
    one = jnp.ones((1, LANES), F32)

    def block_rows(b, at):
        def row(l, at):
            table[0, at] = b
            table[1, at] = l
            return at + 1

        return lax.fori_loop(0, lens[first + b], row, at)

    items = lax.fori_loop(0, count, block_rows, jnp.int32(0))

    def item(i):
        i = jnp.minimum(i, items - 1)
        return table[0, i], table[1, i]

    def fetch(i):
        b, l = item(i)
        slot = i & (RING - 1)
        return pltpu.make_async_copy(geom.at[:, lists[first + b, l]], src.at[slot, pl.ds(0, 7)], sem.at[slot])

    for i in range(AHEAD):
        fetch(jnp.int32(i)).start()
    far[...] = jnp.zeros_like(far)

    def circle(b):
        t = targ[:, pl.ds(pl.multiple_of((first + b) * LANES, LANES), LANES)]
        radius = t[9:10] * KAPPA
        return t[0:3] * KAPPA, radius * t[3:6], 2 * radius * t[3:6], 2 * radius * t[6:9]

    def build(b, carry):
        position, lift, normal, tangent = circle(b)
        origin = jnp.broadcast_to(jnp.mean(position, axis=1, keepdims=True), (3, LANES))
        org[b, 0:3] = origin
        center = position - origin + lift
        for m in range(CHECKS):
            point = center + math.cos(angle(m)) * normal + math.sin(angle(m)) * tangent
            square = total_of(point * point)
            far[0:1] = jnp.maximum(far[0:1], square)
            features = jnp.concatenate([square, point, one, zero, zero, zero], axis=0)
            wts[b, :, m * LANES : (m + 1) * LANES] = stacked(features, LEFT).astype(BF16)
        return carry

    lax.fori_loop(0, count, build, 0)
    out[...] = jnp.zeros_like(out)

    def prepare(i, slot):
        b, _ = item(i)
        g = src[i & (RING - 1), 0:7]
        y = g[0:3] * KAPPA - org[b, 0:3]
        n = g[3:6] * KAPPA
        square = total_of(y * y)
        far[1:2] = jnp.maximum(far[1:2], square)
        for_square = jnp.concatenate([one, -2.0 * y, square, zero, zero, zero], axis=0)
        for_facing = jnp.concatenate([zero, n, -total_of(n * y), zero, zero, zero], axis=0)
        both = jnp.concatenate([stacked(for_square, RIGHT), stacked(for_facing, RIGHT)], axis=0)
        both = both.T.astype(BF16)
        for j in range(8):
            lhs[slot, 32 * j : 32 * j + 16] = both[16 * j : 16 * j + 16, 0:DEPTH]
            lhs[slot, 32 * j + 16 : 32 * j + 32] = both[16 * j : 16 * j + 16, DEPTH : 2 * DEPTH]

    def two_points(b, slot, k):
        return jnp.dot(lhs[slot], wts[b, :, 256 * k : 256 * k + 256], preferred_element_type=F32)

    def flush(i, g):
        b, l = item(i)
        high, low = halves(ups[...] * g[6:7])
        tile_high, tile_low = halves(tile[...])
        left = jnp.concatenate(
            [
                jnp.concatenate([high, high], axis=1),
                jnp.concatenate([low, jnp.zeros_like(low)], axis=1),
            ],
            axis=0,
        )
        right = jnp.concatenate([tile_high, tile_low], axis=0)
        sums = jnp.dot(left, right, preferred_element_type=F32)
        rows = pl.ds(pl.multiple_of(l * NODES, NODES), NODES)
        out[b, rows] = sums[0:NODES] + sums[NODES : 2 * NODES]

    def potential(square, facing, m):
        inverse = lax.rsqrt(square)
        single = jnp.exp2(log_weight(m) - square * inverse) * inverse
        return single + single * (inverse * (inverse + LN2) * facing)

    def step(i, carry):
        slot = i & 1
        fetch(i + 2).wait()
        fetch(i + AHEAD).start()
        last = jnp.maximum(i - 1, 0)
        flush(last, src[last & (RING - 1), 0:7])
        next_b, _ = item(i + 1)
        sums = [None] * 8
        for k in range(CHECKS // 2):
            r = pairs[:, 256 * k : 256 * k + 256]
            for half in range(2):
                cols = slice(LANES * half, LANES * half + LANES)
                for x in range(8):
                    value = potential(r[32 * x : 32 * x + 16, cols], r[32 * x + 16 : 32 * x + 32, cols], 2 * k + half)
                    sums[x] = value if sums[x] is None else sums[x] + value
            pairs[:, 256 * k : 256 * k + 256] = two_points(next_b, 1 - slot, k)
        for x in range(8):
            tile[16 * x : 16 * x + 16] = sums[x]
        prepare(i + 2, slot)
        return carry

    tile[...] = jnp.zeros_like(tile)
    for i in range(2):
        fetch(jnp.int32(i)).wait()
        prepare(jnp.int32(i), i)
    start_b, _ = item(jnp.int32(0))
    for k in range(CHECKS // 2):
        pairs[:, 256 * k : 256 * k + 256] = two_points(start_b, 0, k)
    lax.fori_loop(0, items, step, 0)
    flush(items - 1, src[(items - 1) & (RING - 1), 0:7])
    for i in range(2, AHEAD):
        fetch(items + i).wait()

    @pl.when(jnp.max(far[...]) > REACH * KAPPA * KAPPA)
    def _():
        def slow(i, carry):
            copy = fetch(i)
            copy.start()
            copy.wait()
            g = src[i & (RING - 1), 0:7]
            columns = jnp.concatenate([g, zero], axis=0).T
            y = [columns[:, a : a + 1] * KAPPA for a in range(3)]
            n = [columns[:, a + 3 : a + 4] * KAPPA for a in range(3)]
            position, lift, normal, tangent = circle(item(i)[0])
            center = position + lift
            tile[...] = jnp.zeros_like(tile)
            for m in range(CHECKS):
                point = center + math.cos(angle(m)) * normal + math.sin(angle(m)) * tangent
                for x in range(8):
                    rows = slice(16 * x, 16 * x + 16)
                    d = [point[a : a + 1] - y[a][rows] for a in range(3)]
                    square = d[0] * d[0] + d[1] * d[1] + d[2] * d[2]
                    facing = d[0] * n[0][rows] + d[1] * n[1][rows] + d[2] * n[2][rows]
                    tile[rows] += potential(square, facing, m)
            flush(i, g)
            return carry

        lax.fori_loop(0, items, slow, 0)


def coefficients(lists, lens, targ, ups, geom, first, count):
    pairs = 15 * count
    return pl.pallas_call(
        functools.partial(coefficients_body, first=first, count=count),
        grid_spec=pltpu.PrefetchScalarGridSpec(
            num_scalar_prefetch=2,
            grid=(1,),
            in_specs=[
                pl.BlockSpec(memory_space=pltpu.VMEM),
                pl.BlockSpec(memory_space=pltpu.VMEM),
                pl.BlockSpec(memory_space=pltpu.HBM),
            ],
            out_specs=pl.BlockSpec(memory_space=pltpu.VMEM),
            scratch_shapes=[
                pltpu.VMEM((RING, 8, LANES), F32),
                pltpu.VMEM((count, DEPTH, CHECKS * LANES), BF16),
                pltpu.VMEM((2, 2 * LANES, DEPTH), BF16),
                pltpu.VMEM((LANES, LANES), F32),
                pltpu.VMEM((2 * LANES, CHECKS * LANES), F32),
                pltpu.VMEM((count, 8, LANES), F32),
                pltpu.VMEM((8, LANES), F32),
                pltpu.SMEM((2, 16 * count), jnp.int32),
                pltpu.SemaphoreType.DMA((RING,)),
            ],
        ),
        out_shape=jax.ShapeDtypeStruct((count, 16 * NODES, LANES), F32),
        cost_estimate=pl.CostEstimate(
            flops=pairs * 128 * 128 * 16 * 40, bytes_accessed=2 << 20, transcendentals=pairs * 128 * 128 * 32
        ),
        compiler_params=pltpu.CompilerParams(vmem_limit_bytes=VMEM_KEPT),
        name="coefficients%d" % first,
    )(lists, lens, targ, ups, geom)


def combine_body(lists, *refs, counts):
    parts = len(counts)
    coefs = refs[:parts]
    own, before, behind, out = refs[parts:]

    def nodes(e):
        within = own[jnp.clip(e - 64, 0, 255)]
        edge = jnp.where(e < 64, before[jnp.minimum(e, 63)], behind[jnp.maximum(e - 320, 0)])
        return jnp.where((e >= 64) & (e < 320), within, edge)

    b = 0
    for part, count in zip(coefs, counts):
        for i in range(count):
            high, low = halves(jnp.concatenate([nodes(lists[b, l]) for l in range(16)], axis=0))
            c_high, c_low = halves(part[i].T)
            value = jnp.dot(c_high, high, preferred_element_type=F32)
            value += jnp.dot(c_high, low, preferred_element_type=F32)
            value += jnp.dot(c_low, high, preferred_element_type=F32)
            out[b * LANES : (b + 1) * LANES] = value
            b += 1


def combine(lists, coefs, own, before, behind):
    counts = tuple(c.shape[0] for c in coefs)
    vmem = pl.BlockSpec(memory_space=pltpu.VMEM)
    return pl.pallas_call(
        functools.partial(combine_body, counts=counts),
        grid_spec=pltpu.PrefetchScalarGridSpec(
            num_scalar_prefetch=1,
            grid=(1,),
            in_specs=[vmem] * (len(coefs) + 3),
            out_specs=vmem,
        ),
        out_shape=jax.ShapeDtypeStruct((4 * LANES, LANES), F32),
        cost_estimate=pl.CostEstimate(flops=4 << 24, bytes_accessed=4 << 20, transcendentals=0),
        compiler_params=pltpu.CompilerParams(vmem_limit_bytes=24 << 20),
        name="combine",
    )(lists, *coefs, own, before, behind)


def on_device(dens, upsample, src_geom, targ, lists, lens):
    groups = lax.axis_size("patch")
    ups = upsample.T
    geom = jnp.transpose(src_geom, (1, 0, 2))
    copies = jnp.broadcast_to(dens[None], (8, *dens.shape))
    gathered = lax.all_to_all(copies, "helper", 0, 0, tiled=True).reshape(256, NODES, LANES)
    coefs = [coefficients(lists, lens, targ, ups, geom, 0, 3)]
    gathered, coefs[0] = lax.optimization_barrier((gathered, coefs[0]))
    before = lax.ppermute(gathered[192:], "patch", [(g, (g + 1) % groups) for g in range(groups)])
    behind = lax.ppermute(gathered[:64], "patch", [(g, (g - 1) % groups) for g in range(groups)])
    coefs.append(coefficients(lists, lens, targ, ups, geom, 3, 1))
    return combine(lists, coefs, gathered, before, behind)


def solution(mesh):
    in_specs = (
        P(("patch", "helper"), None, None),
        P(),
        P("patch", None, None),
        P(None, ("patch", "helper")),
        P(("patch", "helper"), None),
        P(("patch", "helper")),
    )
    out_specs = P(("patch", "helper"), None)
    return jax.shard_map(on_device, mesh=mesh, in_specs=in_specs, out_specs=out_specs, check_vma=False)
```

```python
import functools
import math

import jax
import jax.numpy as jnp
from jax import lax
from jax.experimental import pallas as pl
from jax.experimental.pallas import tpu as pltpu
from jax.sharding import PartitionSpec as P

CHECKS = 16
NODES = 16
LANES = 128
F32 = jnp.float32
BF16 = jnp.bfloat16

LN2 = math.log(2.0)
KAPPA = 2.0 / LN2
REACH = 0.5

LEFT = (0, 0, 1, 1, 0, 2)
RIGHT = (0, 1, 0, 1, 2, 0)
DEPTH = 64
UNROLL = 2
TAIL = 8
VMEM_KEPT = 67043328 - 5400000


def angle(m):
    return 2.0 * math.pi * m / CHECKS


def log_weight(m):
    weight = 0.75 / (CHECKS * (1.25 + math.cos(angle(m))))
    return math.log2(weight * KAPPA / (4.0 * math.pi))


def halves(x):
    high = x.astype(BF16)
    return high, (x - high.astype(F32)).astype(BF16)


def thirds(x):
    high = x.astype(BF16).astype(F32)
    rest = x - high
    middle = rest.astype(BF16).astype(F32)
    return high, middle, rest - middle


def stacked(features, order):
    parts = thirds(features)
    rows = [parts[i] for i in order]
    rows.append(jnp.zeros((DEPTH - 8 * len(order), LANES), F32))
    return jnp.concatenate(rows, axis=0)


def total_of(x):
    return jnp.sum(x, axis=0, keepdims=True)


def coefficients_body(lists, lens, targ, ups, geom, out, src, wts, lhs, tile, pairs, org, far, table, sem, *, first, count, tail):
    zero = jnp.zeros((1, LANES), F32)
    one = jnp.ones((1, LANES), F32)

    def fetch(i):
        panel = lists[first + table[0, i], table[1, i]]
        return pltpu.make_async_copy(geom.at[:, panel], src.at[i, pl.ds(0, 7)], sem.at[i])

    def block_rows(b, at):
        def row(l, at):
            table[0, at] = b
            table[1, at] = l
            fetch(at).start()
            return at + 1

        length = lens[first + b]
        cut = length - jnp.minimum(length, TAIL)
        if tail:
            return lax.fori_loop(cut, length, row, at)
        return lax.fori_loop(0, jnp.where(b == count - 1, cut, length), row, at)

    items = lax.fori_loop(0, count, block_rows, jnp.int32(0))

    def used(i):
        return jnp.minimum(i, items - 1)

    far[...] = jnp.zeros_like(far)

    def circle(b):
        t = targ[:, pl.ds(pl.multiple_of((first + b) * LANES, LANES), LANES)]
        radius = t[9:10] * KAPPA
        return t[0:3] * KAPPA, radius * t[3:6], 2 * radius * t[3:6], 2 * radius * t[6:9]

    def build(b, carry):
        position, lift, normal, tangent = circle(b)
        origin = jnp.broadcast_to(jnp.mean(position, axis=1, keepdims=True), (3, LANES))
        org[b, 0:3] = origin
        center = position - origin + lift
        for m in range(CHECKS):
            point = center + math.cos(angle(m)) * normal + math.sin(angle(m)) * tangent
            square = total_of(point * point)
            far[0:1] = jnp.maximum(far[0:1], square)
            features = jnp.concatenate([square, point, one, zero, zero, zero], axis=0)
            wts[b, :, m * LANES : (m + 1) * LANES] = stacked(features, LEFT).astype(BF16)
        return carry

    lax.fori_loop(0, count, build, 0)
    out[...] = jnp.zeros_like(out)

    def arrived(i, carry):
        fetch(i).wait()
        return carry

    lax.fori_loop(0, items, arrived, 0)

    def prepare(i, slot):
        i = used(i)
        b = table[0, i]
        g = src[i, 0:7]
        y = g[0:3] * KAPPA - org[b, 0:3]
        n = g[3:6] * KAPPA
        square = total_of(y * y)
        far[1:2] = jnp.maximum(far[1:2], square)
        for_square = jnp.concatenate([one, -2.0 * y, square, zero, zero, zero], axis=0)
        for_facing = jnp.concatenate([zero, n, -total_of(n * y), zero, zero, zero], axis=0)
        both = jnp.concatenate([stacked(for_square, RIGHT), stacked(for_facing, RIGHT)], axis=0)
        both = both.T.astype(BF16)
        for j in range(8):
            lhs[slot, 32 * j : 32 * j + 16] = both[16 * j : 16 * j + 16, 0:DEPTH]
            lhs[slot, 32 * j + 16 : 32 * j + 32] = both[16 * j : 16 * j + 16, DEPTH : 2 * DEPTH]

    def two_points(b, slot, k):
        return jnp.dot(lhs[slot], wts[b, :, 256 * k : 256 * k + 256], preferred_element_type=F32)

    def flush(i):
        i = used(i)
        b = table[0, i]
        l = table[1, i]
        high, low = halves(ups[...] * src[i, 6:7])
        tile_high, tile_low = halves(tile[...])
        left = jnp.concatenate(
            [
                jnp.concatenate([high, high], axis=1),
                jnp.concatenate([low, jnp.zeros_like(low)], axis=1),
            ],
            axis=0,
        )
        right = jnp.concatenate([tile_high, tile_low], axis=0)
        sums = jnp.dot(left, right, preferred_element_type=F32)
        rows = pl.ds(pl.multiple_of(l * NODES, NODES), NODES)
        out[b, rows] = sums[0:NODES] + sums[NODES : 2 * NODES]

    def potential(square, facing, m):
        inverse = lax.rsqrt(square)
        single = jnp.exp2(log_weight(m) - square * inverse) * inverse
        return single + single * (inverse * (inverse + LN2) * facing)

    def step(i):
        slot = i & 1
        flush(jnp.maximum(i - 1, 0))
        next_b = table[0, used(i + 1)]
        sums = [None] * 8
        for k in range(CHECKS // 2):
            r = pairs[:, 256 * k : 256 * k + 256]
            for half in range(2):
                cols = slice(LANES * half, LANES * half + LANES)
                for x in range(8):
                    value = potential(r[32 * x : 32 * x + 16, cols], r[32 * x + 16 : 32 * x + 32, cols], 2 * k + half)
                    sums[x] = value if sums[x] is None else sums[x] + value
            pairs[:, 256 * k : 256 * k + 256] = two_points(next_b, 1 - slot, k)
        for x in range(8):
            tile[16 * x : 16 * x + 16] = sums[x]
        prepare(i + 2, slot)

    tile[...] = jnp.zeros_like(tile)
    for i in range(2):
        prepare(jnp.int32(i), i)
    start_b = jnp.int32(0)
    for k in range(CHECKS // 2):
        pairs[:, 256 * k : 256 * k + 256] = two_points(start_b, 0, k)
    rounds = (items + 1) >> 1

    def steps(i, carry):
        for j in range(UNROLL):
            step(UNROLL * i + j)
        return carry

    lax.fori_loop(0, rounds, steps, 0)
    flush(items - 1)

    @pl.when(jnp.max(far[...]) > REACH * KAPPA * KAPPA)
    def _():
        def slow(i, carry):
            g = src[i, 0:7]
            columns = jnp.concatenate([g, zero], axis=0).T
            y = [columns[:, a : a + 1] * KAPPA for a in range(3)]
            n = [columns[:, a + 3 : a + 4] * KAPPA for a in range(3)]
            position, lift, normal, tangent = circle(table[0, i])
            center = position + lift
            tile[...] = jnp.zeros_like(tile)
            for m in range(CHECKS):
                point = center + math.cos(angle(m)) * normal + math.sin(angle(m)) * tangent
                for x in range(8):
                    rows = slice(16 * x, 16 * x + 16)
                    d = [point[a : a + 1] - y[a][rows] for a in range(3)]
                    square = d[0] * d[0] + d[1] * d[1] + d[2] * d[2]
                    facing = d[0] * n[0][rows] + d[1] * n[1][rows] + d[2] * n[2][rows]
                    tile[rows] += potential(square, facing, m)
            flush(i)
            return carry

        lax.fori_loop(0, items, slow, 0)


def coefficients(lists, lens, targ, ups, geom, first, count, tail):
    pairs = TAIL if tail else 15 * count - TAIL
    return pl.pallas_call(
        functools.partial(coefficients_body, first=first, count=count, tail=tail),
        grid_spec=pltpu.PrefetchScalarGridSpec(
            num_scalar_prefetch=2,
            grid=(1,),
            in_specs=[
                pl.BlockSpec(memory_space=pltpu.VMEM),
                pl.BlockSpec(memory_space=pltpu.VMEM),
                pl.BlockSpec(memory_space=pltpu.HBM),
            ],
            out_specs=pl.BlockSpec(memory_space=pltpu.VMEM),
            scratch_shapes=[
                pltpu.VMEM((16 * count, 8, LANES), F32),
                pltpu.VMEM((count, DEPTH, CHECKS * LANES), BF16),
                pltpu.VMEM((2, 2 * LANES, DEPTH), BF16),
                pltpu.VMEM((LANES, LANES), F32),
                pltpu.VMEM((2 * LANES, CHECKS * LANES), F32),
                pltpu.VMEM((count, 8, LANES), F32),
                pltpu.VMEM((8, LANES), F32),
                pltpu.SMEM((2, 16 * count), jnp.int32),
                pltpu.SemaphoreType.DMA((16 * count,)),
            ],
        ),
        out_shape=pltpu.VMEM((count, 16 * NODES, LANES), F32),
        cost_estimate=pl.CostEstimate(
            flops=pairs * 128 * 128 * 16 * 40, bytes_accessed=2 << 20, transcendentals=pairs * 128 * 128 * 32
        ),
        compiler_params=pltpu.CompilerParams(vmem_limit_bytes=VMEM_KEPT),
        name="coefficients_%s" % ("tail" if tail else "head"),
    )(lists, lens, targ, ups, geom)


def combine_body(lists, head, tail, own, before, behind, out):
    def nodes(e):
        within = own[jnp.clip(e - 64, 0, 255)]
        edge = jnp.where(e < 64, before[jnp.minimum(e, 63)], behind[jnp.maximum(e - 320, 0)])
        return jnp.where((e >= 64) & (e < 320), within, edge)

    for b in range(4):
        high, low = halves(jnp.concatenate([nodes(lists[b, l]) for l in range(16)], axis=0))
        c = head[b] + tail[0] if b == 3 else head[b]
        c_high, c_low = halves(c.T)
        value = jnp.dot(c_high, high, preferred_element_type=F32)
        value += jnp.dot(c_high, low, preferred_element_type=F32)
        value += jnp.dot(c_low, high, preferred_element_type=F32)
        out[b * LANES : (b + 1) * LANES] = value


def combine(lists, head, tail, own, before, behind):
    vmem = pl.BlockSpec(memory_space=pltpu.VMEM)
    return pl.pallas_call(
        combine_body,
        grid_spec=pltpu.PrefetchScalarGridSpec(
            num_scalar_prefetch=1,
            grid=(1,),
            in_specs=[vmem] * 5,
            out_specs=vmem,
        ),
        out_shape=jax.ShapeDtypeStruct((4 * LANES, LANES), F32),
        cost_estimate=pl.CostEstimate(flops=4 << 24, bytes_accessed=4 << 20, transcendentals=0),
        compiler_params=pltpu.CompilerParams(vmem_limit_bytes=24 << 20),
        name="combine",
    )(lists, head, tail, own, before, behind)


def spread_body(x, out, sem):
    copies = [pltpu.make_async_copy(x, out.at[k], sem.at[k]) for k in range(8)]
    for copy in copies:
        copy.start()
    for copy in copies:
        copy.wait()


def spread(x):
    return pl.pallas_call(
        spread_body,
        in_specs=[pl.BlockSpec(memory_space=pltpu.VMEM)],
        out_specs=pl.BlockSpec(memory_space=pl.ANY),
        out_shape=jax.ShapeDtypeStruct((8, *x.shape), F32),
        scratch_shapes=[pltpu.SemaphoreType.DMA((8,))],
        name="spread",
    )(x)


def on_device(dens, upsample, src_geom, targ, lists, lens):
    groups = lax.axis_size("patch")
    ups = upsample.T
    geom = jnp.transpose(src_geom, (1, 0, 2))
    gathered = lax.all_to_all(spread(dens), "helper", 0, 0, tiled=True).reshape(256, NODES, LANES)
    head = coefficients(lists, lens, targ, ups, geom, 0, 4, False)
    gathered, head = lax.optimization_barrier((gathered, head))
    before = lax.ppermute(gathered[192:], "patch", [(g, (g + 1) % groups) for g in range(groups)])
    behind = lax.ppermute(gathered[:64], "patch", [(g, (g - 1) % groups) for g in range(groups)])
    tail = coefficients(lists, lens, targ, ups, geom, 3, 1, True)
    return combine(lists, head, tail, gathered, before, behind)


def solution(mesh):
    in_specs = (
        P(("patch", "helper"), None, None),
        P(),
        P("patch", None, None),
        P(None, ("patch", "helper")),
        P(("patch", "helper"), None),
        P(("patch", "helper")),
    )
    out_specs = P(("patch", "helper"), None)
    return jax.shard_map(on_device, mesh=mesh, in_specs=in_specs, out_specs=out_specs, check_vma=False)
```

```python
import functools
import math

import jax
import jax.numpy as jnp
from jax import lax
from jax.experimental import pallas as pl
from jax.experimental.pallas import tpu as pltpu
from jax.sharding import PartitionSpec as P

CHECKS = 16
NODES = 16
SLOTS = 16
LANES = 128
F32 = jnp.float32
BF16 = jnp.bfloat16

LN2 = math.log(2.0)
KAPPA = 2.0 / LN2
REACH = 0.5

LEFT = (0, 0, 1, 1, 0, 2)
RIGHT = (0, 1, 0, 1, 2, 0)
DEPTH = 64
TAIL = 24
VMEM_ALL = 67043328
VMEM_KEPT = 24 << 20


def angle(m):
    return 2.0 * math.pi * m / CHECKS


def log_weight(m):
    weight = 0.75 / (CHECKS * (1.25 + math.cos(angle(m))))
    return math.log2(weight * KAPPA / (4.0 * math.pi))


def halves(x):
    high = x.astype(BF16)
    return high, (x - high.astype(F32)).astype(BF16)


def thirds(x):
    high = x.astype(BF16).astype(F32)
    rest = x - high
    middle = rest.astype(BF16).astype(F32)
    return high, middle, rest - middle


def stacked(features, order):
    parts = thirds(features)
    rows = [parts[i] for i in order]
    rows.append(jnp.zeros((DEPTH - 8 * len(order), LANES), F32))
    return jnp.concatenate(rows, axis=0)


def total_of(x):
    return jnp.sum(x, axis=0, keepdims=True)


def circle(targ, b):
    t = targ[:, pl.ds(pl.multiple_of(b * LANES, LANES), LANES)]
    radius = t[9:10] * KAPPA
    return t[0:3] * KAPPA, radius * t[3:6], 2 * radius * t[3:6], 2 * radius * t[6:9]


def spread_body(x, out, sem):
    copies = [pltpu.make_async_copy(x, out.at[k], sem.at[k]) for k in range(8)]
    for copy in copies:
        copy.start()
    for copy in copies:
        copy.wait()


def spread(x):
    return pl.pallas_call(
        spread_body,
        in_specs=[pl.BlockSpec(memory_space=pltpu.VMEM)],
        out_specs=pl.BlockSpec(memory_space=pl.ANY),
        out_shape=jax.ShapeDtypeStruct((8, *x.shape), F32),
        scratch_shapes=[pltpu.SemaphoreType.DMA((8,))],
        name="spread",
    )(x)


def collect(lists, lens, targ_in, ups_in, geom, src, targ, ups, table, sem, sem_panel):
    small = [pltpu.make_async_copy(targ_in, targ, sem.at[0]), pltpu.make_async_copy(ups_in, ups, sem.at[1])]
    for copy in small:
        copy.start()

    def fetch(at):
        panel = geom.at[:, lists[at >> 4, at & 15]]
        return pltpu.make_async_copy(panel, src.at[at, pl.ds(0, 7)], sem_panel.at[at])

    items = jnp.int32(0)
    for b in range(4):

        def row(l, i, b=b):
            table[i] = SLOTS * b + l
            fetch(SLOTS * b + l).start()
            return i + 1

        items = lax.fori_loop(0, lens[b], row, items)
    table[4 * SLOTS] = items
    for copy in small:
        copy.wait()

    def arrived(i, carry):
        fetch(table[i]).wait()
        return carry

    return lambda: lax.fori_loop(0, items, arrived, 0)


def head_body(lists, lens, targ_in, ups_in, geom, out, src, targ, ups, table, *scratch):
    *scratch, sem, sem_panel = scratch
    wait = collect(lists, lens, targ_in, ups_in, geom, src, targ, ups, table, sem, sem_panel)
    coefficients_body(table, src, targ, ups, out, *scratch, tail=False, wait=wait)


def tail_body(table, src, targ, ups, out, *scratch):
    coefficients_body(table, src, targ, ups, out, *scratch, tail=True, wait=None)


def coefficients_body(table, src, targ, ups, out, wts, org, lhs, tile, pairs, far, *, tail, wait):
    every = table[4 * SLOTS]
    late = jnp.minimum(every >> 1, TAIL)
    first, items = (every - late, late) if tail else (0, every - late)

    def entry(i):
        return table[first + jnp.minimum(i, items - 1)]

    out[...] = jnp.zeros_like(out)
    zero = jnp.zeros((1, LANES), F32)
    one = jnp.ones((1, LANES), F32)
    far[...] = jnp.zeros_like(far)

    def build(b, carry):
        position, lift, normal, tangent = circle(targ, b)
        origin = jnp.broadcast_to(jnp.mean(position, axis=1, keepdims=True), (3, LANES))
        org[b, 0:3] = origin
        center = position - origin + lift
        for m in range(CHECKS):
            point = center + math.cos(angle(m)) * normal + math.sin(angle(m)) * tangent
            square = total_of(point * point)
            far[0:1] = jnp.maximum(far[0:1], square)
            features = jnp.concatenate([square, point, one, zero, zero, zero], axis=0)
            wts[b, :, m * LANES : (m + 1) * LANES] = stacked(features, LEFT).astype(BF16)
        return carry

    lax.fori_loop(entry(0) >> 4, (entry(items - 1) >> 4) + 1, build, 0)
    if wait:
        wait()

    def prepare(i, slot):
        at = entry(i)
        g = src[at, 0:7]
        y = g[0:3] * KAPPA - org[at >> 4, 0:3]
        n = g[3:6] * KAPPA
        square = total_of(y * y)
        far[1:2] = jnp.maximum(far[1:2], square)
        for_square = jnp.concatenate([one, -2.0 * y, square, zero, zero, zero], axis=0)
        for_facing = jnp.concatenate([zero, n, -total_of(n * y), zero, zero, zero], axis=0)
        both = jnp.concatenate([stacked(for_square, RIGHT), stacked(for_facing, RIGHT)], axis=0)
        both = both.T.astype(BF16)
        for j in range(8):
            lhs[slot, 32 * j : 32 * j + 16] = both[16 * j : 16 * j + 16, 0:DEPTH]
            lhs[slot, 32 * j + 16 : 32 * j + 32] = both[16 * j : 16 * j + 16, DEPTH : 2 * DEPTH]

    def two_points(b, slot, k):
        return jnp.dot(lhs[slot], wts[b, :, 256 * k : 256 * k + 256], preferred_element_type=F32)

    def flush(i):
        at = entry(i)
        high, low = halves(ups[...] * src[at, 6:7])
        tile_high, tile_low = halves(tile[...])
        left = jnp.concatenate(
            [
                jnp.concatenate([high, high], axis=1),
                jnp.concatenate([low, jnp.zeros_like(low)], axis=1),
            ],
            axis=0,
        )
        right = jnp.concatenate([tile_high, tile_low], axis=0)
        sums = jnp.dot(left, right, preferred_element_type=F32)
        rows = pl.ds(pl.multiple_of((at & 15) * NODES, NODES), NODES)
        out[at >> 4, rows] = sums[0:NODES] + sums[NODES : 2 * NODES]

    def potential(square, facing, m):
        inverse = lax.rsqrt(square)
        single = jnp.exp2(log_weight(m) - square * inverse) * inverse
        return single + single * (inverse * (inverse + LN2) * facing)

    def step(i, slot):
        flush(jnp.maximum(i - 1, 0))
        next_b = entry(i + 1) >> 4
        sums = [None] * 8
        for k in range(CHECKS // 2):
            r = pairs[:, 256 * k : 256 * k + 256]
            for half in range(2):
                cols = slice(LANES * half, LANES * half + LANES)
                for x in range(8):
                    value = potential(r[32 * x : 32 * x + 16, cols], r[32 * x + 16 : 32 * x + 32, cols], 2 * k + half)
                    sums[x] = value if sums[x] is None else sums[x] + value
            pairs[:, 256 * k : 256 * k + 256] = two_points(next_b, 1 - slot, k)
        for x in range(8):
            tile[16 * x : 16 * x + 16] = sums[x]
        prepare(i + 2, slot)

    tile[...] = jnp.zeros_like(tile)
    for i in range(2):
        prepare(i, i)
    for k in range(CHECKS // 2):
        pairs[:, 256 * k : 256 * k + 256] = two_points(entry(0) >> 4, 0, k)

    def steps(i, carry):
        for j in range(2):
            step(2 * i + j, j)
        return carry

    lax.fori_loop(0, (items + 1) >> 1, steps, 0)
    flush(items - 1)

    @pl.when(jnp.max(far[...]) > REACH * KAPPA * KAPPA)
    def _():
        def slow(i, carry):
            at = entry(i)
            columns = jnp.concatenate([src[at, 0:7], zero], axis=0).T
            y = [columns[:, a : a + 1] * KAPPA for a in range(3)]
            n = [columns[:, a + 3 : a + 4] * KAPPA for a in range(3)]
            position, lift, normal, tangent = circle(targ, at >> 4)
            center = position + lift
            tile[...] = jnp.zeros_like(tile)
            for m in range(CHECKS):
                point = center + math.cos(angle(m)) * normal + math.sin(angle(m)) * tangent
                for x in range(8):
                    rows = slice(16 * x, 16 * x + 16)
                    d = [point[a : a + 1] - y[a][rows] for a in range(3)]
                    square = d[0] * d[0] + d[1] * d[1] + d[2] * d[2]
                    facing = d[0] * n[0][rows] + d[1] * n[1][rows] + d[2] * n[2][rows]
                    tile[rows] += potential(square, facing, m)
            flush(i)
            return carry

        lax.fori_loop(0, items, slow, 0)


VMEM = pl.BlockSpec(memory_space=pltpu.VMEM)
KEPT = pl.BlockSpec(memory_space=pl.ANY)
WORK = [
    pltpu.VMEM((4, DEPTH, CHECKS * LANES), BF16),
    pltpu.VMEM((4, 8, LANES), F32),
    pltpu.VMEM((2, 2 * LANES, DEPTH), BF16),
    pltpu.VMEM((LANES, LANES), F32),
    pltpu.VMEM((2 * LANES, CHECKS * LANES), F32),
    pltpu.VMEM((8, LANES), F32),
]
SUMS = pltpu.VMEM((4, SLOTS * NODES, LANES), F32)


def cost(items):
    points = items * 128 * 128 * CHECKS
    return pl.CostEstimate(flops=40 * points, bytes_accessed=2 << 20, transcendentals=2 * points)


def coefficients_head(lists, lens, targ, ups, geom):
    return pl.pallas_call(
        head_body,
        grid_spec=pltpu.PrefetchScalarGridSpec(
            num_scalar_prefetch=2,
            grid=(1,),
            in_specs=[KEPT] * 3,
            out_specs=[VMEM] * 4 + [pl.BlockSpec(memory_space=pltpu.SMEM)],
            scratch_shapes=WORK + [pltpu.SemaphoreType.DMA((2,)), pltpu.SemaphoreType.DMA((4 * SLOTS,))],
        ),
        out_shape=[
            SUMS,
            pltpu.VMEM((4 * SLOTS, 8, LANES), F32),
            pltpu.VMEM(targ.shape, F32),
            pltpu.VMEM(ups.shape, F32),
            jax.ShapeDtypeStruct((4 * SLOTS + 1,), jnp.int32),
        ],
        cost_estimate=cost(60 - TAIL),
        compiler_params=pltpu.CompilerParams(vmem_limit_bytes=VMEM_ALL - 3800000),
        name="coefficients_head",
    )(lists, lens, targ, ups, geom)


def coefficients_tail(table, src, targ, ups):
    return pl.pallas_call(
        tail_body,
        grid_spec=pltpu.PrefetchScalarGridSpec(
            num_scalar_prefetch=1, grid=(1,), in_specs=[VMEM] * 3, out_specs=VMEM, scratch_shapes=WORK
        ),
        out_shape=SUMS,
        cost_estimate=cost(TAIL),
        compiler_params=pltpu.CompilerParams(vmem_limit_bytes=VMEM_KEPT),
        name="coefficients_tail",
    )(table, src, targ, ups)


def combine_body(lists, head, tail, own, before, behind, out):
    def nodes(e):
        within = own[jnp.clip(e - 64, 0, 255)]
        edge = jnp.where(e < 64, before[jnp.minimum(e, 63)], behind[jnp.maximum(e - 320, 0)])
        return jnp.where((e >= 64) & (e < 320), within, edge)

    for b in range(4):
        high, low = halves(jnp.concatenate([nodes(lists[b, l]) for l in range(16)], axis=0))
        c_high, c_low = halves((head[b] + tail[b]).T)
        value = jnp.dot(c_high, high, preferred_element_type=F32)
        value += jnp.dot(c_high, low, preferred_element_type=F32)
        value += jnp.dot(c_low, high, preferred_element_type=F32)
        out[b * LANES : (b + 1) * LANES] = value


def combine(lists, head, tail, own, before, behind):
    vmem = pl.BlockSpec(memory_space=pltpu.VMEM)
    return pl.pallas_call(
        combine_body,
        grid_spec=pltpu.PrefetchScalarGridSpec(
            num_scalar_prefetch=1,
            grid=(1,),
            in_specs=[vmem] * 5,
            out_specs=vmem,
        ),
        out_shape=jax.ShapeDtypeStruct((4 * LANES, LANES), F32),
        cost_estimate=pl.CostEstimate(flops=4 << 24, bytes_accessed=4 << 20, transcendentals=0),
        compiler_params=pltpu.CompilerParams(vmem_limit_bytes=24 << 20),
        name="combine",
    )(lists, head, tail, own, before, behind)


def on_device(dens, upsample, src_geom, targ, lists, lens):
    groups = lax.axis_size("patch")
    geom = jnp.transpose(src_geom, (1, 0, 2))
    gathered = lax.all_to_all(spread(dens), "helper", 0, 0, tiled=True).reshape(256, NODES, LANES)
    head, src, targ, ups, table = coefficients_head(lists, lens, targ, upsample.T, geom)
    gathered, head = lax.optimization_barrier((gathered, head))
    before = lax.ppermute(gathered[192:], "patch", [(g, (g + 1) % groups) for g in range(groups)])
    behind = lax.ppermute(gathered[:64], "patch", [(g, (g - 1) % groups) for g in range(groups)])
    tail = coefficients_tail(table, src, targ, ups)
    return combine(lists, head, tail, gathered, before, behind)


def solution(mesh):
    in_specs = (
        P(("patch", "helper"), None, None),
        P(),
        P("patch", None, None),
        P(None, ("patch", "helper")),
        P(("patch", "helper"), None),
        P(("patch", "helper")),
    )
    out_specs = P(("patch", "helper"), None)
    return jax.shard_map(on_device, mesh=mesh, in_specs=in_specs, out_specs=out_specs, check_vma=False)
```

```python
import functools
import math

import jax
import jax.numpy as jnp
from jax import lax
from jax.experimental import pallas as pl
from jax.experimental.pallas import tpu as pltpu
from jax.sharding import PartitionSpec as P

CHECKS = 16
NODES = 16
SLOTS = 16
LANES = 128
F32 = jnp.float32
BF16 = jnp.bfloat16

LN2 = math.log(2.0)
KAPPA = 2.0 / LN2
REACH = 0.5

LEFT = (0, 0, 1, 1, 0, 2)
RIGHT = (0, 1, 0, 1, 2, 0)
DEPTH = 64
HOLDERS = 0x21304756
VMEM_ALL = 67043328


def angle(m):
    return 2.0 * math.pi * m / CHECKS


def log_weight(m):
    weight = 0.75 / (CHECKS * (1.25 + math.cos(angle(m))))
    return math.log2(weight * KAPPA / (4.0 * math.pi))


def halves(x):
    high = x.astype(BF16)
    return high, (x - high.astype(F32)).astype(BF16)


def thirds(x):
    high = x.astype(BF16).astype(F32)
    rest = x - high
    middle = rest.astype(BF16).astype(F32)
    return high, middle, rest - middle


def stacked(features, order):
    parts = thirds(features)
    rows = [parts[i] for i in order]
    rows.append(jnp.zeros((DEPTH - 8 * len(order), LANES), F32))
    return jnp.concatenate(rows, axis=0)


def total_of(x):
    return jnp.sum(x, axis=0, keepdims=True)


def circle(targ, b):
    t = targ[:, pl.ds(pl.multiple_of(b * LANES, LANES), LANES)]
    radius = t[9:10] * KAPPA
    return t[0:3] * KAPPA, radius * t[3:6], 2 * radius * t[3:6], 2 * radius * t[6:9]


def spread_body(x, out, sem):
    copies = [pltpu.make_async_copy(x, out.at[k], sem.at[k]) for k in range(8)]
    for copy in copies:
        copy.start()
    for copy in copies:
        copy.wait()


def spread(x):
    return pl.pallas_call(
        spread_body,
        in_specs=[pl.BlockSpec(memory_space=pltpu.VMEM)],
        out_specs=pl.BlockSpec(memory_space=pl.ANY),
        out_shape=jax.ShapeDtypeStruct((8, *x.shape), F32),
        scratch_shapes=[pltpu.SemaphoreType.DMA((8,))],
        compiler_params=pltpu.CompilerParams(vmem_limit_bytes=8 << 20),
        name="spread",
    )(x)


def collect(lists, lens, targ_in, ups_in, geom, src, targ, ups, table, sem, sem_panel):
    small = [pltpu.make_async_copy(targ_in, targ, sem.at[0]), pltpu.make_async_copy(ups_in, ups, sem.at[1])]
    for copy in small:
        copy.start()

    def fetch(at):
        panel = geom.at[:, lists[at >> 4, at & 15]]
        return pltpu.make_async_copy(panel, src.at[at, pl.ds(0, 7)], sem_panel.at[at])

    items = jnp.int32(0)
    for b in range(4):

        def row(l, i, b=b):
            table[i] = SLOTS * b + l
            fetch(SLOTS * b + l).start()
            return i + 1

        items = lax.fori_loop(0, lens[b], row, items)
    for copy in small:
        copy.wait()

    def arrived(i, carry):
        fetch(table[i]).wait()
        return carry

    return items, lambda: lax.fori_loop(0, items, arrived, 0)


def coefficients_body(
    lists, lens, targ_in, ups_in, geom, out, src, targ, ups, table, wts, org, lhs, tile, pairs, far, sem, sem_panel
):
    items, wait_for_panels = collect(lists, lens, targ_in, ups_in, geom, src, targ, ups, table, sem, sem_panel)

    def entry(i):
        return table[jnp.minimum(i, items - 1)]

    out[...] = jnp.zeros_like(out)
    zero = jnp.zeros((1, LANES), F32)
    one = jnp.ones((1, LANES), F32)
    far[...] = jnp.zeros_like(far)

    def build(b, carry):
        position, lift, normal, tangent = circle(targ, b)
        origin = jnp.broadcast_to(jnp.mean(position, axis=1, keepdims=True), (3, LANES))
        org[b, 0:3] = origin
        center = position - origin + lift
        for m in range(CHECKS):
            point = center + math.cos(angle(m)) * normal + math.sin(angle(m)) * tangent
            square = total_of(point * point)
            far[0:1] = jnp.maximum(far[0:1], square)
            features = jnp.concatenate([square, point, one, zero, zero, zero], axis=0)
            wts[b, :, m * LANES : (m + 1) * LANES] = stacked(features, LEFT).astype(BF16)
        return carry

    lax.fori_loop(0, 4, build, 0)
    wait_for_panels()

    def prepare(i, slot):
        at = entry(i)
        g = src[at, 0:7]
        y = g[0:3] * KAPPA - org[at >> 4, 0:3]
        n = g[3:6] * KAPPA
        square = total_of(y * y)
        far[1:2] = jnp.maximum(far[1:2], square)
        for_square = jnp.concatenate([one, -2.0 * y, square, zero, zero, zero], axis=0)
        for_facing = jnp.concatenate([zero, n, -total_of(n * y), zero, zero, zero], axis=0)
        both = jnp.concatenate([stacked(for_square, RIGHT), stacked(for_facing, RIGHT)], axis=0)
        both = both.T.astype(BF16)
        for j in range(8):
            lhs[slot, 32 * j : 32 * j + 16] = both[16 * j : 16 * j + 16, 0:DEPTH]
            lhs[slot, 32 * j + 16 : 32 * j + 32] = both[16 * j : 16 * j + 16, DEPTH : 2 * DEPTH]

    def two_points(b, slot, k):
        return jnp.dot(lhs[slot], wts[b, :, 256 * k : 256 * k + 256], preferred_element_type=F32)

    def flush(i):
        at = entry(i)
        high, low = halves(ups[...] * src[at, 6:7])
        tile_high, tile_low = halves(tile[...])
        left = jnp.concatenate(
            [
                jnp.concatenate([high, high], axis=1),
                jnp.concatenate([low, jnp.zeros_like(low)], axis=1),
            ],
            axis=0,
        )
        right = jnp.concatenate([tile_high, tile_low], axis=0)
        sums = jnp.dot(left, right, preferred_element_type=F32)
        rows = pl.ds(pl.multiple_of((at & 15) * NODES, NODES), NODES)
        out[at >> 4, rows] = sums[0:NODES] + sums[NODES : 2 * NODES]

    def potential(square, facing, m):
        inverse = lax.rsqrt(square)
        single = jnp.exp2(log_weight(m) - square * inverse) * inverse
        return single + single * (inverse * (inverse + LN2) * facing)

    def step(i, slot):
        flush(jnp.maximum(i - 1, 0))
        next_b = entry(i + 1) >> 4
        sums = [None] * 8
        for k in range(CHECKS // 2):
            r = pairs[:, 256 * k : 256 * k + 256]
            for half in range(2):
                cols = slice(LANES * half, LANES * half + LANES)
                for x in range(8):
                    value = potential(r[32 * x : 32 * x + 16, cols], r[32 * x + 16 : 32 * x + 32, cols], 2 * k + half)
                    sums[x] = value if sums[x] is None else sums[x] + value
            pairs[:, 256 * k : 256 * k + 256] = two_points(next_b, 1 - slot, k)
        for x in range(8):
            tile[16 * x : 16 * x + 16] = sums[x]
        prepare(i + 2, slot)

    tile[...] = jnp.zeros_like(tile)
    for i in range(2):
        prepare(i, i)
    for k in range(CHECKS // 2):
        pairs[:, 256 * k : 256 * k + 256] = two_points(entry(0) >> 4, 0, k)

    def steps(i, carry):
        for j in range(2):
            step(2 * i + j, j)
        return carry

    lax.fori_loop(0, (items + 1) >> 1, steps, 0)
    flush(items - 1)

    @pl.when(jnp.max(far[...]) > REACH * KAPPA * KAPPA)
    def _():
        def slow(i, carry):
            at = entry(i)
            columns = jnp.concatenate([src[at, 0:7], zero], axis=0).T
            y = [columns[:, a : a + 1] * KAPPA for a in range(3)]
            n = [columns[:, a + 3 : a + 4] * KAPPA for a in range(3)]
            position, lift, normal, tangent = circle(targ, at >> 4)
            center = position + lift
            tile[...] = jnp.zeros_like(tile)
            for m in range(CHECKS):
                point = center + math.cos(angle(m)) * normal + math.sin(angle(m)) * tangent
                for x in range(8):
                    rows = slice(16 * x, 16 * x + 16)
                    d = [point[a : a + 1] - y[a][rows] for a in range(3)]
                    square = d[0] * d[0] + d[1] * d[1] + d[2] * d[2]
                    facing = d[0] * n[0][rows] + d[1] * n[1][rows] + d[2] * n[2][rows]
                    tile[rows] += potential(square, facing, m)
            flush(i)
            return carry

        lax.fori_loop(0, items, slow, 0)


VMEM = pl.BlockSpec(memory_space=pltpu.VMEM)
KEPT = pl.BlockSpec(memory_space=pl.ANY)


def coefficients(lists, lens, targ, ups, geom):
    points = 4 * 15 * 128 * 128 * CHECKS
    return pl.pallas_call(
        coefficients_body,
        grid_spec=pltpu.PrefetchScalarGridSpec(
            num_scalar_prefetch=2,
            grid=(1,),
            in_specs=[KEPT] * 3,
            out_specs=VMEM,
            scratch_shapes=[
                pltpu.VMEM((4 * SLOTS, 8, LANES), F32),
                pltpu.VMEM(targ.shape, F32),
                pltpu.VMEM(ups.shape, F32),
                pltpu.SMEM((4 * SLOTS,), jnp.int32),
                pltpu.VMEM((4, DEPTH, CHECKS * LANES), BF16),
                pltpu.VMEM((4, 8, LANES), F32),
                pltpu.VMEM((2, 2 * LANES, DEPTH), BF16),
                pltpu.VMEM((LANES, LANES), F32),
                pltpu.VMEM((2 * LANES, CHECKS * LANES), F32),
                pltpu.VMEM((8, LANES), F32),
                pltpu.SemaphoreType.DMA((2,)),
                pltpu.SemaphoreType.DMA((4 * SLOTS,)),
            ],
        ),
        out_shape=jax.ShapeDtypeStruct((4, SLOTS * NODES, LANES), F32),
        cost_estimate=pl.CostEstimate(flops=40 * points, bytes_accessed=2 << 20, transcendentals=2 * points),
        compiler_params=pltpu.CompilerParams(vmem_limit_bytes=VMEM_ALL - 3800000),
        name="coefficients",
    )(lists, lens, targ, ups, geom)


def combine_body(lists, coefs, gathered, out):
    def nodes(e):
        chunk = jnp.where(e < 64, e >> 4, 4 + ((e - 320) >> 4))
        holder = (HOLDERS >> (4 * (chunk & 7))) & 7
        inner = (e >= 64) & (e < 320)
        own = jnp.where(inner, e - 64, 0)
        return gathered[jnp.where(inner, own >> 5, holder), jnp.where(inner, own & 31, 32 + (e & 15))]

    for b in range(4):
        high, low = halves(jnp.concatenate([nodes(lists[b, l]) for l in range(SLOTS)], axis=0))
        c_high, c_low = halves(coefs[b].T)
        value = jnp.dot(c_high, high, preferred_element_type=F32)
        value += jnp.dot(c_high, low, preferred_element_type=F32)
        value += jnp.dot(c_low, high, preferred_element_type=F32)
        out[b * LANES : (b + 1) * LANES] = value


def combine(lists, coefs, gathered):
    return pl.pallas_call(
        combine_body,
        grid_spec=pltpu.PrefetchScalarGridSpec(num_scalar_prefetch=1, grid=(1,), in_specs=[VMEM] * 2, out_specs=VMEM),
        out_shape=jax.ShapeDtypeStruct((4 * LANES, LANES), F32),
        cost_estimate=pl.CostEstimate(flops=4 << 24, bytes_accessed=4 << 20, transcendentals=0),
        compiler_params=pltpu.CompilerParams(vmem_limit_bytes=24 << 20),
        name="combine",
    )(lists, coefs, gathered)


def spread_body(x, out, sem):
    copies = [pltpu.make_async_copy(x, out.at[k, pl.ds(0, 32)], sem.at[k]) for k in range(8)]
    for copy in copies:
        copy.start()
    for copy in copies:
        copy.wait()


def spread(x):
    return pl.pallas_call(
        spread_body,
        in_specs=[VMEM],
        out_specs=KEPT,
        out_shape=jax.ShapeDtypeStruct((8, 48, NODES, LANES), F32),
        scratch_shapes=[pltpu.SemaphoreType.DMA((8,))],
        compiler_params=pltpu.CompilerParams(vmem_limit_bytes=8 << 20),
        name="spread",
    )(x)


def spread_edge_body(place, first, second, own, out, sem):
    outer = (place[0] < 2) | (place[0] >= 6)

    def put(x):
        copies = [pltpu.make_async_copy(x, out.at[k, pl.ds(32, 16)], sem.at[k]) for k in range(8)]
        for copy in copies:
            copy.start()
        for copy in copies:
            copy.wait()

    @pl.when(outer)
    def _():
        put(first.at[pl.ds(0, 16)])

    @pl.when(jnp.logical_not(outer))
    def _():
        put(second.at[pl.ds(16, 16)])


def spread_edge(place, first, second, own):
    return pl.pallas_call(
        spread_edge_body,
        grid_spec=pltpu.PrefetchScalarGridSpec(
            num_scalar_prefetch=1,
            grid=(1,),
            in_specs=[VMEM] * 2 + [KEPT],
            out_specs=KEPT,
            scratch_shapes=[pltpu.SemaphoreType.DMA((8,))],
        ),
        out_shape=jax.ShapeDtypeStruct(own.shape, F32),
        input_output_aliases={3: 0},
        compiler_params=pltpu.CompilerParams(vmem_limit_bytes=8 << 20),
        name="spread_edge",
    )(place, first, second, own)


def on_device(dens, upsample, src_geom, targ, lists, lens):
    groups = lax.axis_size("patch")
    geom = jnp.transpose(src_geom, (1, 0, 2))

    def halo(targets):
        moves = []
        for g in range(groups):
            for source, target in zip((6, 7, 0, 1), targets):
                to = g + 1 if source >= 6 else g - 1
                moves.append((8 * g + source, 8 * (to % groups) + target))
        return lax.ppermute(dens, ("patch", "helper"), moves)

    first = halo((6, 7, 0, 1))
    second = halo((5, 4, 3, 2))
    place = lax.axis_index("helper").astype(jnp.int32).reshape(1)
    copies = spread_edge(place, first, second, spread(dens))
    gathered = lax.all_to_all(copies, "helper", 0, 0, tiled=True)
    coefs = coefficients(lists, lens, targ, upsample.T, geom)
    return combine(lists, coefs, gathered)


def solution(mesh):
    in_specs = (
        P(("patch", "helper"), None, None),
        P(),
        P("patch", None, None),
        P(None, ("patch", "helper")),
        P(("patch", "helper"), None),
        P(("patch", "helper")),
    )
    out_specs = P(("patch", "helper"), None)
    return jax.shard_map(on_device, mesh=mesh, in_specs=in_specs, out_specs=out_specs, check_vma=False)
```

```python
import functools
import math

import jax
import jax.numpy as jnp
from jax import lax
from jax.experimental import pallas as pl
from jax.experimental.pallas import tpu as pltpu
from jax.sharding import PartitionSpec as P

CHECKS = 16
NODES = 16
SLOTS = 16
LANES = 128
F32 = jnp.float32
BF16 = jnp.bfloat16

LN2 = math.log(2.0)
KAPPA = 2.0 / LN2
REACH = 0.5

LEFT = (0, 0, 1, 1, 0, 2)
RIGHT = (0, 1, 0, 1, 2, 0)
DEPTH = 64
HEAD = 3
HOLDERS = 0x21304756
VMEM_ALL = 67043328
VMEM_KEPT = 24 << 20


def angle(m):
    return 2.0 * math.pi * m / CHECKS


def log_weight(m):
    weight = 0.75 / (CHECKS * (1.25 + math.cos(angle(m))))
    return math.log2(weight * KAPPA / (4.0 * math.pi))


def halves(x):
    high = x.astype(BF16)
    return high, (x - high.astype(F32)).astype(BF16)


def thirds(x):
    high = x.astype(BF16).astype(F32)
    rest = x - high
    middle = rest.astype(BF16).astype(F32)
    return high, middle, rest - middle


def stacked(features, order):
    parts = thirds(features)
    rows = [parts[i] for i in order]
    rows.append(jnp.zeros((DEPTH - 8 * len(order), LANES), F32))
    return jnp.concatenate(rows, axis=0)


def total_of(x):
    return jnp.sum(x, axis=0, keepdims=True)


def circle(targ, b):
    t = targ[:, pl.ds(pl.multiple_of(b * LANES, LANES), LANES)]
    radius = t[9:10] * KAPPA
    return t[0:3] * KAPPA, radius * t[3:6], 2 * radius * t[3:6], 2 * radius * t[6:9]


def spread_body(x, out, sem):
    copies = [pltpu.make_async_copy(x, out.at[k], sem.at[k]) for k in range(8)]
    for copy in copies:
        copy.start()
    for copy in copies:
        copy.wait()


def spread(x):
    return pl.pallas_call(
        spread_body,
        in_specs=[pl.BlockSpec(memory_space=pltpu.VMEM)],
        out_specs=pl.BlockSpec(memory_space=pl.ANY),
        out_shape=jax.ShapeDtypeStruct((8, *x.shape), F32),
        scratch_shapes=[pltpu.SemaphoreType.DMA((8,))],
        name="spread",
    )(x)


def collect(lists, lens, targ_in, ups_in, geom, src, src_tail, targ, ups, table, sem, sem_panel):
    small = [pltpu.make_async_copy(targ_in, targ, sem.at[0]), pltpu.make_async_copy(ups_in, ups, sem.at[1])]
    for copy in small:
        copy.start()

    def fetch(b, l):
        panel = geom.at[:, lists[b, l]]
        to = src.at[SLOTS * b + l] if b < HEAD else src_tail.at[SLOTS * (b - HEAD) + l]
        return pltpu.make_async_copy(panel, to.at[pl.ds(0, 7)], sem_panel.at[SLOTS * b + l])

    items = jnp.int32(0)
    for b in range(4):

        def row(l, i, b=b):
            table[i] = SLOTS * b + l
            fetch(b, l).start()
            return i + 1

        table[4 * SLOTS + b] = items
        items = lax.fori_loop(0, lens[b], row, items)
    table[4 * SLOTS + 4] = items
    for copy in small:
        copy.wait()

    def wait():
        for b in range(4):

            def arrived(l, carry, b=b):
                fetch(b, l).wait()
                return carry

            lax.fori_loop(0, lens[b], arrived, 0)

    return wait


def head_body(lists, lens, targ_in, ups_in, geom, out, src_tail, targ, ups, table, *scratch):
    *scratch, src, sem, sem_panel = scratch
    wait = collect(lists, lens, targ_in, ups_in, geom, src, src_tail, targ, ups, table, sem, sem_panel)
    coefficients_body(table, src, targ, ups, out, *scratch, tail=False, wait=wait)


def tail_body(table, src, targ, ups, out, *scratch):
    coefficients_body(table, src, targ, ups, out, *scratch, tail=True, wait=None)


def coefficients_body(table, src, targ, ups, out, wts, org, lhs, tile, pairs, far, *, tail, wait):
    first_block, blocks = (HEAD, 4 - HEAD) if tail else (0, HEAD)
    first = table[4 * SLOTS + first_block]
    items = table[4 * SLOTS + first_block + blocks] - first

    def entry(i):
        return table[first + jnp.minimum(i, items - 1)]

    out[...] = jnp.zeros_like(out)
    zero = jnp.zeros((1, LANES), F32)
    one = jnp.ones((1, LANES), F32)
    far[...] = jnp.zeros_like(far)

    def build(b, carry):
        position, lift, normal, tangent = circle(targ, b)
        origin = jnp.broadcast_to(jnp.mean(position, axis=1, keepdims=True), (3, LANES))
        org[b, 0:3] = origin
        center = position - origin + lift
        for m in range(CHECKS):
            point = center + math.cos(angle(m)) * normal + math.sin(angle(m)) * tangent
            square = total_of(point * point)
            far[0:1] = jnp.maximum(far[0:1], square)
            features = jnp.concatenate([square, point, one, zero, zero, zero], axis=0)
            wts[b, :, m * LANES : (m + 1) * LANES] = stacked(features, LEFT).astype(BF16)
        return carry

    lax.fori_loop(first_block, first_block + blocks, build, 0)
    if wait:
        wait()

    def prepare(i, slot):
        at = entry(i)
        g = src[at - SLOTS * first_block, 0:7]
        y = g[0:3] * KAPPA - org[at >> 4, 0:3]
        n = g[3:6] * KAPPA
        square = total_of(y * y)
        far[1:2] = jnp.maximum(far[1:2], square)
        for_square = jnp.concatenate([one, -2.0 * y, square, zero, zero, zero], axis=0)
        for_facing = jnp.concatenate([zero, n, -total_of(n * y), zero, zero, zero], axis=0)
        both = jnp.concatenate([stacked(for_square, RIGHT), stacked(for_facing, RIGHT)], axis=0)
        both = both.T.astype(BF16)
        for j in range(8):
            lhs[slot, 32 * j : 32 * j + 16] = both[16 * j : 16 * j + 16, 0:DEPTH]
            lhs[slot, 32 * j + 16 : 32 * j + 32] = both[16 * j : 16 * j + 16, DEPTH : 2 * DEPTH]

    def two_points(b, slot, k):
        return jnp.dot(lhs[slot], wts[b, :, 256 * k : 256 * k + 256], preferred_element_type=F32)

    def flush(i):
        at = entry(i)
        high, low = halves(ups[...] * src[at - SLOTS * first_block, 6:7])
        tile_high, tile_low = halves(tile[...])
        left = jnp.concatenate(
            [
                jnp.concatenate([high, high], axis=1),
                jnp.concatenate([low, jnp.zeros_like(low)], axis=1),
            ],
            axis=0,
        )
        right = jnp.concatenate([tile_high, tile_low], axis=0)
        sums = jnp.dot(left, right, preferred_element_type=F32)
        rows = pl.ds(pl.multiple_of((at & 15) * NODES, NODES), NODES)
        out[(at >> 4) - first_block, rows] = sums[0:NODES] + sums[NODES : 2 * NODES]

    def potential(square, facing, m):
        inverse = lax.rsqrt(square)
        single = jnp.exp2(log_weight(m) - square * inverse) * inverse
        return single + single * (inverse * (inverse + LN2) * facing)

    def step(i, slot):
        flush(jnp.maximum(i - 1, 0))
        next_b = entry(i + 1) >> 4
        sums = [None] * 8
        for k in range(CHECKS // 2):
            r = pairs[:, 256 * k : 256 * k + 256]
            for half in range(2):
                cols = slice(LANES * half, LANES * half + LANES)
                for x in range(8):
                    value = potential(r[32 * x : 32 * x + 16, cols], r[32 * x + 16 : 32 * x + 32, cols], 2 * k + half)
                    sums[x] = value if sums[x] is None else sums[x] + value
            pairs[:, 256 * k : 256 * k + 256] = two_points(next_b, 1 - slot, k)
        for x in range(8):
            tile[16 * x : 16 * x + 16] = sums[x]
        prepare(i + 2, slot)

    tile[...] = jnp.zeros_like(tile)
    for i in range(2):
        prepare(i, i)
    for k in range(CHECKS // 2):
        pairs[:, 256 * k : 256 * k + 256] = two_points(entry(0) >> 4, 0, k)

    def steps(i, carry):
        for j in range(2):
            step(2 * i + j, j)
        return carry

    lax.fori_loop(0, (items + 1) >> 1, steps, 0)
    flush(items - 1)

    @pl.when(jnp.max(far[...]) > REACH * KAPPA * KAPPA)
    def _():
        def slow(i, carry):
            at = entry(i)
            columns = jnp.concatenate([src[at - SLOTS * first_block, 0:7], zero], axis=0).T
            y = [columns[:, a : a + 1] * KAPPA for a in range(3)]
            n = [columns[:, a + 3 : a + 4] * KAPPA for a in range(3)]
            position, lift, normal, tangent = circle(targ, at >> 4)
            center = position + lift
            tile[...] = jnp.zeros_like(tile)
            for m in range(CHECKS):
                point = center + math.cos(angle(m)) * normal + math.sin(angle(m)) * tangent
                for x in range(8):
                    rows = slice(16 * x, 16 * x + 16)
                    d = [point[a : a + 1] - y[a][rows] for a in range(3)]
                    square = d[0] * d[0] + d[1] * d[1] + d[2] * d[2]
                    facing = d[0] * n[0][rows] + d[1] * n[1][rows] + d[2] * n[2][rows]
                    tile[rows] += potential(square, facing, m)
            flush(i)
            return carry

        lax.fori_loop(0, items, slow, 0)


VMEM = pl.BlockSpec(memory_space=pltpu.VMEM)
KEPT = pl.BlockSpec(memory_space=pl.ANY)
WORK = [
    pltpu.VMEM((4, DEPTH, CHECKS * LANES), BF16),
    pltpu.VMEM((4, 8, LANES), F32),
    pltpu.VMEM((2, 2 * LANES, DEPTH), BF16),
    pltpu.VMEM((LANES, LANES), F32),
    pltpu.VMEM((2 * LANES, CHECKS * LANES), F32),
    pltpu.VMEM((8, LANES), F32),
]


def sums_shape(blocks):
    return blocks, SLOTS * NODES, LANES


def cost(items):
    points = items * 128 * 128 * CHECKS
    return pl.CostEstimate(flops=40 * points, bytes_accessed=2 << 20, transcendentals=2 * points)


def coefficients_head(lists, lens, targ, ups, geom):
    return pl.pallas_call(
        head_body,
        grid_spec=pltpu.PrefetchScalarGridSpec(
            num_scalar_prefetch=2,
            grid=(1,),
            in_specs=[KEPT] * 3,
            out_specs=[VMEM] * 4 + [pl.BlockSpec(memory_space=pltpu.SMEM)],
            scratch_shapes=WORK
            + [pltpu.VMEM((SLOTS * HEAD, 8, LANES), F32), pltpu.SemaphoreType.DMA((2,)), pltpu.SemaphoreType.DMA((4 * SLOTS,))],
        ),
        out_shape=[
            jax.ShapeDtypeStruct(sums_shape(HEAD), F32),
            pltpu.VMEM((SLOTS * (4 - HEAD), 8, LANES), F32),
            pltpu.VMEM(targ.shape, F32),
            pltpu.VMEM(ups.shape, F32),
            jax.ShapeDtypeStruct((4 * SLOTS + 5,), jnp.int32),
        ],
        cost_estimate=cost(15 * HEAD),
        compiler_params=pltpu.CompilerParams(vmem_limit_bytes=VMEM_ALL - 3800000),
        name="coefficients_head",
    )(lists, lens, targ, ups, geom)


def coefficients_tail(table, src, targ, ups):
    return pl.pallas_call(
        tail_body,
        grid_spec=pltpu.PrefetchScalarGridSpec(
            num_scalar_prefetch=1, grid=(1,), in_specs=[VMEM] * 3, out_specs=VMEM, scratch_shapes=WORK
        ),
        out_shape=pltpu.VMEM(sums_shape(4 - HEAD), F32),
        cost_estimate=cost(60 - 15 * HEAD),
        compiler_params=pltpu.CompilerParams(vmem_limit_bytes=VMEM_KEPT),
        name="coefficients_tail",
    )(table, src, targ, ups)


def combine_body(lists, head, tail, own, edge, out):
    def nodes(e):
        chunk = jnp.where(e < 64, e >> 4, 4 + ((e - 320) >> 4))
        holder = (HOLDERS >> (4 * (chunk & 7))) & 7
        within = own[jnp.clip(e - 64, 0, 255)]
        return jnp.where((e >= 64) & (e < 320), within, edge[16 * holder + (e & 15)])

    for b in range(4):
        high, low = halves(jnp.concatenate([nodes(lists[b, l]) for l in range(SLOTS)], axis=0))
        c = head[b] if b < HEAD else tail[b - HEAD]
        c_high, c_low = halves(c.T)
        value = jnp.dot(c_high, high, preferred_element_type=F32)
        value += jnp.dot(c_high, low, preferred_element_type=F32)
        value += jnp.dot(c_low, high, preferred_element_type=F32)
        out[b * LANES : (b + 1) * LANES] = value


def combine(lists, head, tail, own, edge):
    return pl.pallas_call(
        combine_body,
        grid_spec=pltpu.PrefetchScalarGridSpec(num_scalar_prefetch=1, grid=(1,), in_specs=[VMEM] * 4, out_specs=VMEM),
        out_shape=jax.ShapeDtypeStruct((4 * LANES, LANES), F32),
        cost_estimate=pl.CostEstimate(flops=4 << 24, bytes_accessed=4 << 20, transcendentals=0),
        compiler_params=pltpu.CompilerParams(vmem_limit_bytes=24 << 20),
        name="combine",
    )(lists, head, tail, own, edge)


def spread_body(x, out, sem):
    copies = [pltpu.make_async_copy(x, out.at[k], sem.at[k]) for k in range(8)]
    for copy in copies:
        copy.start()
    for copy in copies:
        copy.wait()


def spread(x):
    return pl.pallas_call(
        spread_body,
        in_specs=[VMEM],
        out_specs=KEPT,
        out_shape=jax.ShapeDtypeStruct((8, *x.shape), F32),
        scratch_shapes=[pltpu.SemaphoreType.DMA((8,))],
        compiler_params=pltpu.CompilerParams(vmem_limit_bytes=VMEM_ALL - 3800000),
        name="spread",
    )(x)


def spread_edge_body(place, first, second, out, sem):
    outer = (place[0] < 2) | (place[0] >= 6)

    @pl.when(outer)
    def _():
        spread_body(first.at[pl.ds(0, 16)], out, sem)

    @pl.when(jnp.logical_not(outer))
    def _():
        spread_body(second.at[pl.ds(16, 16)], out, sem)


def spread_edge(place, first, second):
    return pl.pallas_call(
        spread_edge_body,
        grid_spec=pltpu.PrefetchScalarGridSpec(
            num_scalar_prefetch=1,
            grid=(1,),
            in_specs=[VMEM] * 2,
            out_specs=KEPT,
            scratch_shapes=[pltpu.SemaphoreType.DMA((8,))],
        ),
        out_shape=jax.ShapeDtypeStruct((8, 16, NODES, LANES), F32),
        compiler_params=pltpu.CompilerParams(vmem_limit_bytes=VMEM_ALL - 3200000),
        name="spread_edge",
    )(place, first, second)


def on_device(dens, upsample, src_geom, targ, lists, lens):
    groups = lax.axis_size("patch")
    geom = jnp.transpose(src_geom, (1, 0, 2))
    own = lax.all_to_all(spread(dens), "helper", 0, 0, tiled=True)

    def halo(targets):
        moves = []
        for g in range(groups):
            for source, target in zip((6, 7, 0, 1), targets):
                to = g + 1 if source >= 6 else g - 1
                moves.append((8 * g + source, 8 * (to % groups) + target))
        return lax.ppermute(dens, ("patch", "helper"), moves)

    first = halo((6, 7, 0, 1))
    second = halo((5, 4, 3, 2))
    place = lax.axis_index("helper").astype(jnp.int32).reshape(1)
    head, src, targ, ups, table = coefficients_head(lists, lens, targ, upsample.T, geom)
    first, second, own, src = lax.optimization_barrier((first, second, own, src))
    edge = lax.all_to_all(spread_edge(place, first, second), "helper", 0, 0, tiled=True)
    tail = coefficients_tail(table, src, targ, ups)
    return combine(lists, head, tail, own.reshape(256, NODES, LANES), edge.reshape(128, NODES, LANES))


def solution(mesh):
    in_specs = (
        P(("patch", "helper"), None, None),
        P(),
        P("patch", None, None),
        P(None, ("patch", "helper")),
        P(("patch", "helper"), None),
        P(("patch", "helper")),
    )
    out_specs = P(("patch", "helper"), None)
    return jax.shard_map(on_device, mesh=mesh, in_specs=in_specs, out_specs=out_specs, check_vma=False)
```

```python
import functools
import math

import jax
import jax.numpy as jnp
from jax import lax
from jax.experimental import pallas as pl
from jax.experimental.pallas import tpu as pltpu
from jax.sharding import PartitionSpec as P

CHECKS = 16
NODES = 16
SLOTS = 16
LANES = 128
F32 = jnp.float32
BF16 = jnp.bfloat16

LN2 = math.log(2.0)
KAPPA = 2.0 / LN2
REACH = 0.5

LEFT = (0, 0, 1, 1, 0, 2)
RIGHT = (0, 1, 0, 1, 2, 0)
DEPTH = 64
TAIL = 16
VMEM_ALL = 67043328
VMEM_KEPT = 24 << 20


def angle(m):
    return 2.0 * math.pi * m / CHECKS


def log_weight(m):
    weight = 0.75 / (CHECKS * (1.25 + math.cos(angle(m))))
    return math.log2(weight * KAPPA / (4.0 * math.pi))


def halves(x):
    high = x.astype(BF16)
    return high, (x - high.astype(F32)).astype(BF16)


def thirds(x):
    high = x.astype(BF16).astype(F32)
    rest = x - high
    middle = rest.astype(BF16).astype(F32)
    return high, middle, rest - middle


def stacked(features, order):
    parts = thirds(features)
    rows = [parts[i] for i in order]
    rows.append(jnp.zeros((DEPTH - 8 * len(order), LANES), F32))
    return jnp.concatenate(rows, axis=0)


def total_of(x):
    return jnp.sum(x, axis=0, keepdims=True)


def circle(targ, b):
    t = targ[:, pl.ds(pl.multiple_of(b * LANES, LANES), LANES)]
    radius = t[9:10] * KAPPA
    return t[0:3] * KAPPA, radius * t[3:6], 2 * radius * t[3:6], 2 * radius * t[6:9]


def spread_body(x, out, sem):
    copies = [pltpu.make_async_copy(x, out.at[k], sem.at[k]) for k in range(8)]
    for copy in copies:
        copy.start()
    for copy in copies:
        copy.wait()


def spread(x):
    return pl.pallas_call(
        spread_body,
        in_specs=[pl.BlockSpec(memory_space=pltpu.VMEM)],
        out_specs=pl.BlockSpec(memory_space=pl.ANY),
        out_shape=jax.ShapeDtypeStruct((8, *x.shape), F32),
        scratch_shapes=[pltpu.SemaphoreType.DMA((8,))],
        name="spread",
    )(x)


def collect(lists, lens, targ_in, ups_in, geom, src, targ, ups, table, sem, sem_panel):
    small = [pltpu.make_async_copy(targ_in, targ, sem.at[0]), pltpu.make_async_copy(ups_in, ups, sem.at[1])]
    for copy in small:
        copy.start()

    def fetch(at):
        panel = geom.at[:, lists[at >> 4, at & 15]]
        return pltpu.make_async_copy(panel, src.at[at, pl.ds(0, 7)], sem_panel.at[at])

    items = jnp.int32(0)
    for b in range(4):

        def row(l, i, b=b):
            table[i] = SLOTS * b + l
            fetch(SLOTS * b + l).start()
            return i + 1

        items = lax.fori_loop(0, lens[b], row, items)
    table[4 * SLOTS] = items
    for copy in small:
        copy.wait()

    def arrived(i, carry):
        fetch(table[i]).wait()
        return carry

    return lambda: lax.fori_loop(0, items, arrived, 0)


def head_body(lists, lens, targ_in, ups_in, geom, out, src, targ, ups, table, *scratch):
    *scratch, sem, sem_panel = scratch
    wait = collect(lists, lens, targ_in, ups_in, geom, src, targ, ups, table, sem, sem_panel)
    coefficients_body(table, src, targ, ups, out, *scratch, tail=False, wait=wait)


def tail_body(table, src, targ, ups, out, *scratch):
    coefficients_body(table, src, targ, ups, out, *scratch, tail=True, wait=None)


def coefficients_body(table, src, targ, ups, out, wts, org, lhs, tile, pairs, far, *, tail, wait):
    every = table[4 * SLOTS]
    late = jnp.minimum(every >> 1, TAIL)
    first, items = (every - late, late) if tail else (0, every - late)

    def entry(i):
        return table[first + jnp.minimum(i, items - 1)]

    out[...] = jnp.zeros_like(out)
    zero = jnp.zeros((1, LANES), F32)
    one = jnp.ones((1, LANES), F32)
    far[...] = jnp.zeros_like(far)

    def build(b, carry):
        position, lift, normal, tangent = circle(targ, b)
        origin = jnp.broadcast_to(jnp.mean(position, axis=1, keepdims=True), (3, LANES))
        org[b, 0:3] = origin
        center = position - origin + lift
        for m in range(CHECKS):
            point = center + math.cos(angle(m)) * normal + math.sin(angle(m)) * tangent
            square = total_of(point * point)
            far[0:1] = jnp.maximum(far[0:1], square)
            features = jnp.concatenate([square, point, one, zero, zero, zero], axis=0)
            wts[b, :, m * LANES : (m + 1) * LANES] = stacked(features, LEFT).astype(BF16)
        return carry

    lax.fori_loop(entry(0) >> 4, (entry(items - 1) >> 4) + 1, build, 0)
    if wait:
        wait()

    def prepare(i, slot):
        at = entry(i)
        g = src[at, 0:7]
        y = g[0:3] * KAPPA - org[at >> 4, 0:3]
        n = g[3:6] * KAPPA
        square = total_of(y * y)
        far[1:2] = jnp.maximum(far[1:2], square)
        for_square = jnp.concatenate([one, -2.0 * y, square, zero, zero, zero], axis=0)
        for_facing = jnp.concatenate([zero, n, -total_of(n * y), zero, zero, zero], axis=0)
        both = jnp.concatenate([stacked(for_square, RIGHT), stacked(for_facing, RIGHT)], axis=0)
        both = both.T.astype(BF16)
        for j in range(8):
            lhs[slot, 32 * j : 32 * j + 16] = both[16 * j : 16 * j + 16, 0:DEPTH]
            lhs[slot, 32 * j + 16 : 32 * j + 32] = both[16 * j : 16 * j + 16, DEPTH : 2 * DEPTH]

    def two_points(b, slot, k):
        return jnp.dot(lhs[slot], wts[b, :, 256 * k : 256 * k + 256], preferred_element_type=F32)

    def flush(i):
        at = entry(i)
        high, low = halves(ups[...] * src[at, 6:7])
        tile_high, tile_low = halves(tile[...])
        left = jnp.concatenate(
            [
                jnp.concatenate([high, high], axis=1),
                jnp.concatenate([low, jnp.zeros_like(low)], axis=1),
            ],
            axis=0,
        )
        right = jnp.concatenate([tile_high, tile_low], axis=0)
        sums = jnp.dot(left, right, preferred_element_type=F32)
        rows = pl.ds(pl.multiple_of((at & 15) * NODES, NODES), NODES)
        out[at >> 4, rows] = sums[0:NODES] + sums[NODES : 2 * NODES]

    def potential(square, facing, m):
        inverse = lax.rsqrt(square)
        single = jnp.exp2(log_weight(m) - square * inverse) * inverse
        return single + single * (inverse * (inverse + LN2) * facing)

    def step(i, slot):
        flush(jnp.maximum(i - 1, 0))
        next_b = entry(i + 1) >> 4
        sums = [None] * 8
        for k in range(CHECKS // 2):
            r = pairs[:, 256 * k : 256 * k + 256]
            for half in range(2):
                cols = slice(LANES * half, LANES * half + LANES)
                for x in range(8):
                    value = potential(r[32 * x : 32 * x + 16, cols], r[32 * x + 16 : 32 * x + 32, cols], 2 * k + half)
                    sums[x] = value if sums[x] is None else sums[x] + value
            pairs[:, 256 * k : 256 * k + 256] = two_points(next_b, 1 - slot, k)
        for x in range(8):
            tile[16 * x : 16 * x + 16] = sums[x]
        prepare(i + 2, slot)

    tile[...] = jnp.zeros_like(tile)
    for i in range(2):
        prepare(i, i)
    for k in range(CHECKS // 2):
        pairs[:, 256 * k : 256 * k + 256] = two_points(entry(0) >> 4, 0, k)

    def steps(i, carry):
        for j in range(2):
            step(2 * i + j, j)
        return carry

    lax.fori_loop(0, (items + 1) >> 1, steps, 0)
    flush(items - 1)

    @pl.when(jnp.max(far[...]) > REACH * KAPPA * KAPPA)
    def _():
        def slow(i, carry):
            at = entry(i)
            columns = jnp.concatenate([src[at, 0:7], zero], axis=0).T
            y = [columns[:, a : a + 1] * KAPPA for a in range(3)]
            n = [columns[:, a + 3 : a + 4] * KAPPA for a in range(3)]
            position, lift, normal, tangent = circle(targ, at >> 4)
            center = position + lift
            tile[...] = jnp.zeros_like(tile)
            for m in range(CHECKS):
                point = center + math.cos(angle(m)) * normal + math.sin(angle(m)) * tangent
                for x in range(8):
                    rows = slice(16 * x, 16 * x + 16)
                    d = [point[a : a + 1] - y[a][rows] for a in range(3)]
                    square = d[0] * d[0] + d[1] * d[1] + d[2] * d[2]
                    facing = d[0] * n[0][rows] + d[1] * n[1][rows] + d[2] * n[2][rows]
                    tile[rows] += potential(square, facing, m)
            flush(i)
            return carry

        lax.fori_loop(0, items, slow, 0)


VMEM = pl.BlockSpec(memory_space=pltpu.VMEM)
KEPT = pl.BlockSpec(memory_space=pl.ANY)
WORK = [
    pltpu.VMEM((4, DEPTH, CHECKS * LANES), BF16),
    pltpu.VMEM((4, 8, LANES), F32),
    pltpu.VMEM((2, 2 * LANES, DEPTH), BF16),
    pltpu.VMEM((LANES, LANES), F32),
    pltpu.VMEM((2 * LANES, CHECKS * LANES), F32),
    pltpu.VMEM((8, LANES), F32),
]
SUMS = pltpu.VMEM((4, SLOTS * NODES, LANES), F32)


def cost(items):
    points = items * 128 * 128 * CHECKS
    return pl.CostEstimate(flops=40 * points, bytes_accessed=2 << 20, transcendentals=2 * points)


def coefficients_head(lists, lens, targ, ups, geom):
    return pl.pallas_call(
        head_body,
        grid_spec=pltpu.PrefetchScalarGridSpec(
            num_scalar_prefetch=2,
            grid=(1,),
            in_specs=[KEPT] * 3,
            out_specs=[VMEM] * 4 + [pl.BlockSpec(memory_space=pltpu.SMEM)],
            scratch_shapes=WORK + [pltpu.SemaphoreType.DMA((2,)), pltpu.SemaphoreType.DMA((4 * SLOTS,))],
        ),
        out_shape=[
            SUMS,
            pltpu.VMEM((4 * SLOTS, 8, LANES), F32),
            pltpu.VMEM(targ.shape, F32),
            pltpu.VMEM(ups.shape, F32),
            jax.ShapeDtypeStruct((4 * SLOTS + 1,), jnp.int32),
        ],
        cost_estimate=cost(60 - TAIL),
        compiler_params=pltpu.CompilerParams(vmem_limit_bytes=VMEM_ALL - 3800000),
        name="coefficients_head",
    )(lists, lens, targ, ups, geom)


def coefficients_tail(table, src, targ, ups):
    return pl.pallas_call(
        tail_body,
        grid_spec=pltpu.PrefetchScalarGridSpec(
            num_scalar_prefetch=1, grid=(1,), in_specs=[VMEM] * 3, out_specs=VMEM, scratch_shapes=WORK
        ),
        out_shape=SUMS,
        cost_estimate=cost(TAIL),
        compiler_params=pltpu.CompilerParams(vmem_limit_bytes=VMEM_KEPT),
        name="coefficients_tail",
    )(table, src, targ, ups)


def combine_body(lists, odd, head, tail, own, across, beside, out):
    def nodes(e):
        within = own[jnp.clip(e - 64, 0, 255)]
        at = jnp.where(e < 64, e, e - 320) & 63
        edge = jnp.where((e < 64) == (odd[0] == 0), across[at], beside[at])
        return jnp.where((e >= 64) & (e < 320), within, edge)

    for b in range(4):
        high, low = halves(jnp.concatenate([nodes(lists[b, l]) for l in range(SLOTS)], axis=0))
        c_high, c_low = halves((head[b] + tail[b]).T)
        value = jnp.dot(c_high, high, preferred_element_type=F32)
        value += jnp.dot(c_high, low, preferred_element_type=F32)
        value += jnp.dot(c_low, high, preferred_element_type=F32)
        out[b * LANES : (b + 1) * LANES] = value


def combine(lists, odd, head, tail, own, across, beside):
    return pl.pallas_call(
        combine_body,
        grid_spec=pltpu.PrefetchScalarGridSpec(num_scalar_prefetch=2, grid=(1,), in_specs=[VMEM] * 5, out_specs=VMEM),
        out_shape=jax.ShapeDtypeStruct((4 * LANES, LANES), F32),
        cost_estimate=pl.CostEstimate(flops=4 << 24, bytes_accessed=4 << 20, transcendentals=0),
        compiler_params=pltpu.CompilerParams(vmem_limit_bytes=24 << 20),
        name="combine",
    )(lists, odd, head, tail, own, across, beside)


def on_device(dens, upsample, src_geom, targ, lists, lens):
    groups = lax.axis_size("patch")
    geom = jnp.transpose(src_geom, (1, 0, 2))
    gathered = lax.all_to_all(spread(dens), "helper", 0, 0, tiled=True).reshape(256, NODES, LANES)
    head, src, targ, ups, table = coefficients_head(lists, lens, targ, upsample.T, geom)
    gathered, head = lax.optimization_barrier((gathered, head))
    odd = lax.axis_index("patch").astype(jnp.int32) & 1
    far_edge = lax.dynamic_slice_in_dim(gathered, 192 * odd, 64)
    near_edge = lax.dynamic_slice_in_dim(gathered, 192 - 192 * odd, 64)
    across = lax.ppermute(far_edge, "patch", [(g, (g + 2 * (g % 2) - 1) % groups) for g in range(groups)])
    beside = lax.ppermute(near_edge, "patch", [(g, g ^ 1) for g in range(groups)])
    tail = coefficients_tail(table, src, targ, ups)
    return combine(lists, odd.reshape(1), head, tail, gathered, across, beside)


def solution(mesh):
    in_specs = (
        P(("patch", "helper"), None, None),
        P(),
        P("patch", None, None),
        P(None, ("patch", "helper")),
        P(("patch", "helper"), None),
        P(("patch", "helper")),
    )
    out_specs = P(("patch", "helper"), None)
    return jax.shard_map(on_device, mesh=mesh, in_specs=in_specs, out_specs=out_specs, check_vma=False)
```

```python
import functools
import math

import jax
import jax.numpy as jnp
from jax import lax
from jax.experimental import pallas as pl
from jax.experimental.pallas import tpu as pltpu
from jax.sharding import PartitionSpec as P

CHECKS = 16
NODES = 16
SLOTS = 16
LANES = 128
F32 = jnp.float32
BF16 = jnp.bfloat16

LN2 = math.log(2.0)
KAPPA = 2.0 / LN2
REACH = 0.5

LEFT = (0, 0, 1, 1, 0, 2)
RIGHT = (0, 1, 0, 1, 2, 0)
DEPTH = 64
TAIL = 16
VMEM_ALL = 67043328
VMEM_KEPT = 24 << 20


def angle(m):
    return 2.0 * math.pi * m / CHECKS


def log_weight(m):
    weight = 0.75 / (CHECKS * (1.25 + math.cos(angle(m))))
    return math.log2(weight * KAPPA / (4.0 * math.pi))


def halves(x):
    high = x.astype(BF16)
    return high, (x - high.astype(F32)).astype(BF16)


def thirds(x):
    high = x.astype(BF16).astype(F32)
    rest = x - high
    middle = rest.astype(BF16).astype(F32)
    return high, middle, rest - middle


def stacked(features, order):
    parts = thirds(features)
    rows = [parts[i] for i in order]
    rows.append(jnp.zeros((DEPTH - 8 * len(order), LANES), F32))
    return jnp.concatenate(rows, axis=0)


def total_of(x):
    return jnp.sum(x, axis=0, keepdims=True)


def circle(targ, b):
    t = targ[:, pl.ds(pl.multiple_of(b * LANES, LANES), LANES)]
    radius = t[9:10] * KAPPA
    return t[0:3] * KAPPA, radius * t[3:6], 2 * radius * t[3:6], 2 * radius * t[6:9]


def spread_body(x, out, sem):
    copies = [pltpu.make_async_copy(x, out.at[k], sem.at[k]) for k in range(8)]
    for copy in copies:
        copy.start()
    for copy in copies:
        copy.wait()


def spread(x):
    return pl.pallas_call(
        spread_body,
        in_specs=[pl.BlockSpec(memory_space=pltpu.VMEM)],
        out_specs=pl.BlockSpec(memory_space=pl.ANY),
        out_shape=jax.ShapeDtypeStruct((8, *x.shape), F32),
        scratch_shapes=[pltpu.SemaphoreType.DMA((8,))],
        name="spread",
    )(x)


def collect(lists, lens, targ_in, ups_in, geom, src, targ, ups, table, sem, sem_panel):
    small = [pltpu.make_async_copy(targ_in, targ, sem.at[0]), pltpu.make_async_copy(ups_in, ups, sem.at[1])]
    for copy in small:
        copy.start()

    def fetch(at):
        panel = geom.at[:, lists[at >> 4, at & 15]]
        return pltpu.make_async_copy(panel, src.at[at, pl.ds(0, 7)], sem_panel.at[at])

    items = jnp.int32(0)
    for b in range(4):

        def row(l, i, b=b):
            table[i] = SLOTS * b + l
            fetch(SLOTS * b + l).start()
            return i + 1

        items = lax.fori_loop(0, lens[b], row, items)
    table[4 * SLOTS] = items
    for copy in small:
        copy.wait()

    def arrived(i, carry):
        fetch(table[i]).wait()
        return carry

    return lambda: lax.fori_loop(0, items, arrived, 0)


def head_body(lists, lens, targ_in, ups_in, geom, out, src, targ, ups, table, *scratch):
    *scratch, sem, sem_panel = scratch
    wait = collect(lists, lens, targ_in, ups_in, geom, src, targ, ups, table, sem, sem_panel)
    coefficients_body(table, src, targ, ups, out, *scratch, tail=False, wait=wait)


def tail_body(table, src, targ, ups, out, *scratch):
    coefficients_body(table, src, targ, ups, out, *scratch, tail=True, wait=None)


def coefficients_body(table, src, targ, ups, out, wts, org, lhs, tile, pairs, far, *, tail, wait):
    every = table[4 * SLOTS]
    late = jnp.minimum(every >> 1, TAIL)
    first, items = (every - late, late) if tail else (0, every - late)

    def entry(i):
        return table[first + jnp.minimum(i, items - 1)]

    out[...] = jnp.zeros_like(out)
    zero = jnp.zeros((1, LANES), F32)
    one = jnp.ones((1, LANES), F32)
    far[...] = jnp.zeros_like(far)

    def build(b, carry):
        position, lift, normal, tangent = circle(targ, b)
        origin = jnp.broadcast_to(jnp.mean(position, axis=1, keepdims=True), (3, LANES))
        org[b, 0:3] = origin
        center = position - origin + lift
        for m in range(CHECKS):
            point = center + math.cos(angle(m)) * normal + math.sin(angle(m)) * tangent
            square = total_of(point * point)
            far[0:1] = jnp.maximum(far[0:1], square)
            features = jnp.concatenate([square, point, one, zero, zero, zero], axis=0)
            wts[b, :, m * LANES : (m + 1) * LANES] = stacked(features, LEFT).astype(BF16)
        return carry

    lax.fori_loop(entry(0) >> 4, (entry(items - 1) >> 4) + 1, build, 0)
    if wait:
        wait()

    def prepare(i, slot):
        at = entry(i)
        g = src[at, 0:7]
        y = g[0:3] * KAPPA - org[at >> 4, 0:3]
        n = g[3:6] * KAPPA
        square = total_of(y * y)
        far[1:2] = jnp.maximum(far[1:2], square)
        for_square = jnp.concatenate([one, -2.0 * y, square, zero, zero, zero], axis=0)
        for_facing = jnp.concatenate([zero, n, -total_of(n * y), zero, zero, zero], axis=0)
        both = jnp.concatenate([stacked(for_square, RIGHT), stacked(for_facing, RIGHT)], axis=0)
        both = both.T.astype(BF16)
        for j in range(8):
            lhs[slot, 32 * j : 32 * j + 16] = both[16 * j : 16 * j + 16, 0:DEPTH]
            lhs[slot, 32 * j + 16 : 32 * j + 32] = both[16 * j : 16 * j + 16, DEPTH : 2 * DEPTH]

    def two_points(b, slot, k):
        return jnp.dot(lhs[slot], wts[b, :, 256 * k : 256 * k + 256], preferred_element_type=F32)

    def flush(i):
        at = entry(i)
        high, low = halves(ups[...] * src[at, 6:7])
        tile_high, tile_low = halves(tile[...])
        left = jnp.concatenate(
            [
                jnp.concatenate([high, high], axis=1),
                jnp.concatenate([low, jnp.zeros_like(low)], axis=1),
            ],
            axis=0,
        )
        right = jnp.concatenate([tile_high, tile_low], axis=0)
        sums = jnp.dot(left, right, preferred_element_type=F32)
        rows = pl.ds(pl.multiple_of((at & 15) * NODES, NODES), NODES)
        out[at >> 4, rows] = sums[0:NODES] + sums[NODES : 2 * NODES]

    def potential(square, facing, m):
        inverse = lax.rsqrt(square)
        single = jnp.exp2(log_weight(m) - square * inverse) * inverse
        return single + single * (inverse * (inverse + LN2) * facing)

    def step(i, slot):
        flush(jnp.maximum(i - 1, 0))
        next_b = entry(i + 1) >> 4
        sums = [None] * 8
        for k in range(CHECKS // 2):
            r = pairs[:, 256 * k : 256 * k + 256]
            for half in range(2):
                cols = slice(LANES * half, LANES * half + LANES)
                for x in range(8):
                    value = potential(r[32 * x : 32 * x + 16, cols], r[32 * x + 16 : 32 * x + 32, cols], 2 * k + half)
                    sums[x] = value if sums[x] is None else sums[x] + value
            pairs[:, 256 * k : 256 * k + 256] = two_points(next_b, 1 - slot, k)
        for x in range(8):
            tile[16 * x : 16 * x + 16] = sums[x]
        prepare(i + 2, slot)

    tile[...] = jnp.zeros_like(tile)
    for i in range(2):
        prepare(i, i)
    for k in range(CHECKS // 2):
        pairs[:, 256 * k : 256 * k + 256] = two_points(entry(0) >> 4, 0, k)

    def steps(i, carry):
        for j in range(2):
            step(2 * i + j, j)
        return carry

    lax.fori_loop(0, (items + 1) >> 1, steps, 0)
    flush(items - 1)

    @pl.when(jnp.max(far[...]) > REACH * KAPPA * KAPPA)
    def _():
        def slow(i, carry):
            at = entry(i)
            columns = jnp.concatenate([src[at, 0:7], zero], axis=0).T
            y = [columns[:, a : a + 1] * KAPPA for a in range(3)]
            n = [columns[:, a + 3 : a + 4] * KAPPA for a in range(3)]
            position, lift, normal, tangent = circle(targ, at >> 4)
            center = position + lift
            tile[...] = jnp.zeros_like(tile)
            for m in range(CHECKS):
                point = center + math.cos(angle(m)) * normal + math.sin(angle(m)) * tangent
                for x in range(8):
                    rows = slice(16 * x, 16 * x + 16)
                    d = [point[a : a + 1] - y[a][rows] for a in range(3)]
                    square = d[0] * d[0] + d[1] * d[1] + d[2] * d[2]
                    facing = d[0] * n[0][rows] + d[1] * n[1][rows] + d[2] * n[2][rows]
                    tile[rows] += potential(square, facing, m)
            flush(i)
            return carry

        lax.fori_loop(0, items, slow, 0)


VMEM = pl.BlockSpec(memory_space=pltpu.VMEM)
KEPT = pl.BlockSpec(memory_space=pl.ANY)
WORK = [
    pltpu.VMEM((4, DEPTH, CHECKS * LANES), BF16),
    pltpu.VMEM((4, 8, LANES), F32),
    pltpu.VMEM((2, 2 * LANES, DEPTH), BF16),
    pltpu.VMEM((LANES, LANES), F32),
    pltpu.VMEM((2 * LANES, CHECKS * LANES), F32),
    pltpu.VMEM((8, LANES), F32),
]
SUMS = pltpu.VMEM((4, SLOTS * NODES, LANES), F32)


def cost(items):
    points = items * 128 * 128 * CHECKS
    return pl.CostEstimate(flops=40 * points, bytes_accessed=2 << 20, transcendentals=2 * points)


def coefficients_head(lists, lens, targ, ups, geom):
    return pl.pallas_call(
        head_body,
        grid_spec=pltpu.PrefetchScalarGridSpec(
            num_scalar_prefetch=2,
            grid=(1,),
            in_specs=[KEPT] * 3,
            out_specs=[VMEM] * 4 + [pl.BlockSpec(memory_space=pltpu.SMEM)],
            scratch_shapes=WORK + [pltpu.SemaphoreType.DMA((2,)), pltpu.SemaphoreType.DMA((4 * SLOTS,))],
        ),
        out_shape=[
            SUMS,
            pltpu.VMEM((4 * SLOTS, 8, LANES), F32),
            pltpu.VMEM(targ.shape, F32),
            pltpu.VMEM(ups.shape, F32),
            jax.ShapeDtypeStruct((4 * SLOTS + 1,), jnp.int32),
        ],
        cost_estimate=cost(60 - TAIL),
        compiler_params=pltpu.CompilerParams(vmem_limit_bytes=VMEM_ALL - 3800000),
        name="coefficients_head",
    )(lists, lens, targ, ups, geom)


def coefficients_tail(table, src, targ, ups):
    return pl.pallas_call(
        tail_body,
        grid_spec=pltpu.PrefetchScalarGridSpec(
            num_scalar_prefetch=1, grid=(1,), in_specs=[VMEM] * 3, out_specs=VMEM, scratch_shapes=WORK
        ),
        out_shape=SUMS,
        cost_estimate=cost(TAIL),
        compiler_params=pltpu.CompilerParams(vmem_limit_bytes=VMEM_KEPT),
        name="coefficients_tail",
    )(table, src, targ, ups)


def combine_body(lists, head, tail, own, across, beside, out, kept, sem):
    side = 1 - 2 * (lax.axis_index("patch") & 1)

    def nodes(e):
        which = ((e - 64) >> 8) * side
        edge = jnp.where(which < 0, across[e & 63], beside[e & 63])
        return jnp.where(which == 0, own[(e - 64) & 255], edge)

    stores = []
    for b in range(4):
        high, low = halves(jnp.concatenate([nodes(lists[b, l]) for l in range(SLOTS)], axis=0))
        c_high, c_low = halves((head[b] + tail[b]).T)
        value = jnp.dot(c_high, high, preferred_element_type=F32)
        value += jnp.dot(c_high, low, preferred_element_type=F32)
        value += jnp.dot(c_low, high, preferred_element_type=F32)
        kept[b] = value
        stores.append(pltpu.make_async_copy(kept.at[b], out.at[pl.ds(b * LANES, LANES)], sem.at[b]))
        stores[b].start()
    for store in stores:
        store.wait()


def combine(lists, head, tail, own, across, beside):
    return pl.pallas_call(
        combine_body,
        grid_spec=pltpu.PrefetchScalarGridSpec(
            num_scalar_prefetch=1,
            grid=(1,),
            in_specs=[VMEM] * 5,
            out_specs=KEPT,
            scratch_shapes=[pltpu.VMEM((4, LANES, LANES), F32), pltpu.SemaphoreType.DMA((4,))],
        ),
        out_shape=jax.ShapeDtypeStruct((4 * LANES, LANES), F32),
        cost_estimate=pl.CostEstimate(flops=4 << 24, bytes_accessed=4 << 20, transcendentals=0),
        compiler_params=pltpu.CompilerParams(vmem_limit_bytes=24 << 20),
        name="combine",
    )(lists, head, tail, own, across, beside)


def on_device(dens, upsample, src_geom, targ, lists, lens):
    groups = lax.axis_size("patch")
    geom = jnp.transpose(src_geom, (1, 0, 2))
    gathered = lax.all_to_all(spread(dens), "helper", 0, 0, tiled=True).reshape(256, NODES, LANES)
    head, src, targ, ups, table = coefficients_head(lists, lens, targ, upsample.T, geom)
    gathered, head = lax.optimization_barrier((gathered, head))
    odd = lax.axis_index("patch").astype(jnp.int32) & 1
    far_edge = lax.dynamic_slice_in_dim(gathered, 192 * odd, 64)
    near_edge = lax.dynamic_slice_in_dim(gathered, 192 - 192 * odd, 64)
    across = lax.ppermute(far_edge, "patch", [(g, (g + 2 * (g % 2) - 1) % groups) for g in range(groups)])
    beside = lax.ppermute(near_edge, "patch", [(g, g ^ 1) for g in range(groups)])
    tail = coefficients_tail(table, src, targ, ups)
    return combine(lists, head, tail, gathered, across, beside)


def solution(mesh):
    in_specs = (
        P(("patch", "helper"), None, None),
        P(),
        P("patch", None, None),
        P(None, ("patch", "helper")),
        P(("patch", "helper"), None),
        P(("patch", "helper")),
    )
    out_specs = P(("patch", "helper"), None)
    return jax.shard_map(on_device, mesh=mesh, in_specs=in_specs, out_specs=out_specs, check_vma=False)
```

```python
import functools
import math

import jax
import jax.numpy as jnp
from jax import lax
from jax.experimental import pallas as pl
from jax.experimental.pallas import tpu as pltpu
from jax.sharding import PartitionSpec as P

CHECKS = 16
NODES = 16
SLOTS = 16
LANES = 128
F32 = jnp.float32
BF16 = jnp.bfloat16

LN2 = math.log(2.0)
KAPPA = 2.0 / LN2
REACH = 0.5

LEFT = (0, 0, 1, 1, 0, 2)
RIGHT = (0, 1, 0, 1, 2, 0)
DEPTH = 64
TAIL = 16
VMEM_ALL = 67043328
VMEM_KEPT = 24 << 20


def angle(m):
    return 2.0 * math.pi * m / CHECKS


def log_weight(m):
    weight = 0.75 / (CHECKS * (1.25 + math.cos(angle(m))))
    return math.log2(weight * KAPPA / (4.0 * math.pi))


def halves(x):
    high = x.astype(BF16)
    return high, (x - high.astype(F32)).astype(BF16)


def thirds(x):
    high = x.astype(BF16).astype(F32)
    rest = x - high
    middle = rest.astype(BF16).astype(F32)
    return high, middle, rest - middle


def stacked(features, order):
    parts = thirds(features)
    rows = [parts[i] for i in order]
    rows.append(jnp.zeros((DEPTH - 8 * len(order), LANES), F32))
    return jnp.concatenate(rows, axis=0)


def total_of(x):
    return jnp.sum(x, axis=0, keepdims=True)


def circle(targ, b):
    t = targ[:, pl.ds(pl.multiple_of(b * LANES, LANES), LANES)]
    radius = t[9:10] * KAPPA
    return t[0:3] * KAPPA, radius * t[3:6], 2 * radius * t[3:6], 2 * radius * t[6:9]


def spread_body(x, out, sem):
    copies = [pltpu.make_async_copy(x, out.at[k], sem.at[k]) for k in range(8)]
    for copy in copies:
        copy.start()
    for copy in copies:
        copy.wait()


def spread(x):
    return pl.pallas_call(
        spread_body,
        in_specs=[pl.BlockSpec(memory_space=pltpu.VMEM)],
        out_specs=pl.BlockSpec(memory_space=pl.ANY),
        out_shape=jax.ShapeDtypeStruct((8, *x.shape), F32),
        scratch_shapes=[pltpu.SemaphoreType.DMA((8,))],
        name="spread",
    )(x)


def collect(lists, lens, targ_in, ups_in, geom, src, targ, ups, table, sem, sem_panel):
    small = [pltpu.make_async_copy(targ_in, targ, sem.at[0]), pltpu.make_async_copy(ups_in, ups, sem.at[1])]
    for copy in small:
        copy.start()

    def fetch(at):
        panel = geom.at[:, lists[at >> 4, at & 15]]
        return pltpu.make_async_copy(panel, src.at[at, pl.ds(0, 7)], sem_panel.at[at])

    items = jnp.int32(0)
    for b in range(4):

        def row(l, i, b=b):
            table[i] = SLOTS * b + l
            fetch(SLOTS * b + l).start()
            return i + 1

        items = lax.fori_loop(0, lens[b], row, items)
    table[4 * SLOTS] = items
    for copy in small:
        copy.wait()

    def arrived(i, carry):
        fetch(table[i]).wait()
        return carry

    return lambda: lax.fori_loop(0, items, arrived, 0)


def head_body(lists, lens, targ_in, ups_in, geom, out, src, targ, ups, table, *scratch):
    *scratch, sem, sem_panel = scratch
    wait = collect(lists, lens, targ_in, ups_in, geom, src, targ, ups, table, sem, sem_panel)
    coefficients_body(table, src, targ, ups, out, *scratch, tail=False, wait=wait)


def tail_body(table, src, targ, ups, out, *scratch):
    coefficients_body(table, src, targ, ups, out, *scratch, tail=True, wait=None)


def coefficients_body(table, src, targ, ups, out, wts, org, lhs, tile, pairs, far, *, tail, wait):
    every = table[4 * SLOTS]
    late = jnp.minimum(every >> 1, TAIL)
    first, items = (every - late, late) if tail else (0, every - late)

    def entry(i):
        return table[first + jnp.minimum(i, items - 1)]

    out[...] = jnp.zeros_like(out)
    zero = jnp.zeros((1, LANES), F32)
    one = jnp.ones((1, LANES), F32)
    far[...] = jnp.zeros_like(far)

    def build(b, carry):
        position, lift, normal, tangent = circle(targ, b)
        origin = jnp.broadcast_to(jnp.mean(position, axis=1, keepdims=True), (3, LANES))
        org[b, 0:3] = origin
        center = position - origin + lift
        for m in range(CHECKS):
            point = center + math.cos(angle(m)) * normal + math.sin(angle(m)) * tangent
            square = total_of(point * point)
            far[0:1] = jnp.maximum(far[0:1], square)
            features = jnp.concatenate([square, point, one, zero, zero, zero], axis=0)
            wts[b, :, m * LANES : (m + 1) * LANES] = stacked(features, LEFT).astype(BF16)
        return carry

    lax.fori_loop(entry(0) >> 4, (entry(items - 1) >> 4) + 1, build, 0)
    if wait:
        wait()

    def prepare(i, slot):
        at = entry(i)
        g = src[at, 0:7]
        y = g[0:3] * KAPPA - org[at >> 4, 0:3]
        n = g[3:6] * KAPPA
        square = total_of(y * y)
        far[1:2] = jnp.maximum(far[1:2], square)
        for_square = jnp.concatenate([one, -2.0 * y, square, zero, zero, zero], axis=0)
        for_facing = jnp.concatenate([zero, n, -total_of(n * y), zero, zero, zero], axis=0)
        both = jnp.concatenate([stacked(for_square, RIGHT), stacked(for_facing, RIGHT)], axis=0)
        both = both.T.astype(BF16)
        for j in range(8):
            lhs[slot, 32 * j : 32 * j + 16] = both[16 * j : 16 * j + 16, 0:DEPTH]
            lhs[slot, 32 * j + 16 : 32 * j + 32] = both[16 * j : 16 * j + 16, DEPTH : 2 * DEPTH]

    def two_points(b, slot, k):
        return jnp.dot(lhs[slot], wts[b, :, 256 * k : 256 * k + 256], preferred_element_type=F32)

    def flush(i):
        at = entry(i)
        high, low = halves(ups[...] * src[at, 6:7])
        tile_high, tile_low = halves(tile[...])
        left = jnp.concatenate(
            [
                jnp.concatenate([high, high], axis=1),
                jnp.concatenate([low, jnp.zeros_like(low)], axis=1),
            ],
            axis=0,
        )
        right = jnp.concatenate([tile_high, tile_low], axis=0)
        sums = jnp.dot(left, right, preferred_element_type=F32)
        rows = pl.ds(pl.multiple_of((at & 15) * NODES, NODES), NODES)
        out[at >> 4, rows] = sums[0:NODES] + sums[NODES : 2 * NODES]

    def potential(square, facing, m):
        inverse = lax.rsqrt(square)
        single = jnp.exp2(log_weight(m) - square * inverse) * inverse
        return single + single * (inverse * (inverse + LN2) * facing)

    def step(i, slot):
        flush(jnp.maximum(i - 1, 0))
        next_b = entry(i + 1) >> 4
        sums = [None] * 8
        for k in range(CHECKS // 2):
            r = pairs[:, 256 * k : 256 * k + 256]
            for half in range(2):
                cols = slice(LANES * half, LANES * half + LANES)
                for x in range(8):
                    value = potential(r[32 * x : 32 * x + 16, cols], r[32 * x + 16 : 32 * x + 32, cols], 2 * k + half)
                    sums[x] = value if sums[x] is None else sums[x] + value
            pairs[:, 256 * k : 256 * k + 256] = two_points(next_b, 1 - slot, k)
        for x in range(8):
            tile[16 * x : 16 * x + 16] = sums[x]
        prepare(i + 2, slot)

    tile[...] = jnp.zeros_like(tile)
    for i in range(2):
        prepare(i, i)
    for k in range(CHECKS // 2):
        pairs[:, 256 * k : 256 * k + 256] = two_points(entry(0) >> 4, 0, k)

    def steps(i, carry):
        for j in range(2):
            step(2 * i + j, j)
        return carry

    lax.fori_loop(0, (items + 1) >> 1, steps, 0)
    flush(items - 1)

    @pl.when(jnp.max(far[...]) > REACH * KAPPA * KAPPA)
    def _():
        def slow(i, carry):
            at = entry(i)
            columns = jnp.concatenate([src[at, 0:7], zero], axis=0).T
            y = [columns[:, a : a + 1] * KAPPA for a in range(3)]
            n = [columns[:, a + 3 : a + 4] * KAPPA for a in range(3)]
            position, lift, normal, tangent = circle(targ, at >> 4)
            center = position + lift
            tile[...] = jnp.zeros_like(tile)
            for m in range(CHECKS):
                point = center + math.cos(angle(m)) * normal + math.sin(angle(m)) * tangent
                for x in range(8):
                    rows = slice(16 * x, 16 * x + 16)
                    d = [point[a : a + 1] - y[a][rows] for a in range(3)]
                    square = d[0] * d[0] + d[1] * d[1] + d[2] * d[2]
                    facing = d[0] * n[0][rows] + d[1] * n[1][rows] + d[2] * n[2][rows]
                    tile[rows] += potential(square, facing, m)
            flush(i)
            return carry

        lax.fori_loop(0, items, slow, 0)


VMEM = pl.BlockSpec(memory_space=pltpu.VMEM)
KEPT = pl.BlockSpec(memory_space=pl.ANY)
WORK = [
    pltpu.VMEM((4, DEPTH, CHECKS * LANES), BF16),
    pltpu.VMEM((4, 8, LANES), F32),
    pltpu.VMEM((2, 2 * LANES, DEPTH), BF16),
    pltpu.VMEM((LANES, LANES), F32),
    pltpu.VMEM((2 * LANES, CHECKS * LANES), F32),
    pltpu.VMEM((8, LANES), F32),
]
SUMS = pltpu.VMEM((4, SLOTS * NODES, LANES), F32)


def cost(items):
    points = items * 128 * 128 * CHECKS
    return pl.CostEstimate(flops=40 * points, bytes_accessed=2 << 20, transcendentals=2 * points)


def coefficients_head(lists, lens, targ, ups, geom):
    return pl.pallas_call(
        head_body,
        grid_spec=pltpu.PrefetchScalarGridSpec(
            num_scalar_prefetch=2,
            grid=(1,),
            in_specs=[KEPT] * 3,
            out_specs=[VMEM] * 4 + [pl.BlockSpec(memory_space=pltpu.SMEM)],
            scratch_shapes=WORK + [pltpu.SemaphoreType.DMA((2,)), pltpu.SemaphoreType.DMA((4 * SLOTS,))],
        ),
        out_shape=[
            SUMS,
            pltpu.VMEM((4 * SLOTS, 8, LANES), F32),
            pltpu.VMEM(targ.shape, F32),
            pltpu.VMEM(ups.shape, F32),
            jax.ShapeDtypeStruct((4 * SLOTS + 1,), jnp.int32),
        ],
        cost_estimate=cost(60 - TAIL),
        compiler_params=pltpu.CompilerParams(vmem_limit_bytes=VMEM_ALL - 3800000),
        name="coefficients_head",
    )(lists, lens, targ, ups, geom)


def coefficients_tail(table, src, targ, ups):
    return pl.pallas_call(
        tail_body,
        grid_spec=pltpu.PrefetchScalarGridSpec(
            num_scalar_prefetch=1, grid=(1,), in_specs=[VMEM] * 3, out_specs=VMEM, scratch_shapes=WORK
        ),
        out_shape=SUMS,
        cost_estimate=cost(TAIL),
        compiler_params=pltpu.CompilerParams(vmem_limit_bytes=VMEM_KEPT),
        name="coefficients_tail",
    )(table, src, targ, ups)


def combine_body(lists, head, tail, own, across, across_too, beside, out, kept, sem):
    side = 1 - 2 * (lax.axis_index("patch") & 1)

    def nodes(e):
        which = ((e - 64) >> 8) * side
        over = jnp.where((e & 32) == 0, across[e & 31], across_too[e & 31])
        edge = jnp.where(which < 0, over, beside[e & 63])
        return jnp.where(which == 0, own[(e - 64) & 255], edge)

    stores = []
    for b in range(4):
        high, low = halves(jnp.concatenate([nodes(lists[b, l]) for l in range(SLOTS)], axis=0))
        c_high, c_low = halves((head[b] + tail[b]).T)
        value = jnp.dot(c_high, high, preferred_element_type=F32)
        value += jnp.dot(c_high, low, preferred_element_type=F32)
        value += jnp.dot(c_low, high, preferred_element_type=F32)
        kept[b] = value
        stores.append(pltpu.make_async_copy(kept.at[b], out.at[pl.ds(b * LANES, LANES)], sem.at[b]))
        stores[b].start()
    for store in stores:
        store.wait()


def combine(lists, head, tail, own, across, across_too, beside):
    return pl.pallas_call(
        combine_body,
        grid_spec=pltpu.PrefetchScalarGridSpec(
            num_scalar_prefetch=1,
            grid=(1,),
            in_specs=[VMEM] * 6,
            out_specs=KEPT,
            scratch_shapes=[pltpu.VMEM((4, LANES, LANES), F32), pltpu.SemaphoreType.DMA((4,))],
        ),
        out_shape=jax.ShapeDtypeStruct((4 * LANES, LANES), F32),
        cost_estimate=pl.CostEstimate(flops=4 << 24, bytes_accessed=4 << 20, transcendentals=0),
        compiler_params=pltpu.CompilerParams(vmem_limit_bytes=24 << 20),
        name="combine",
    )(lists, head, tail, own, across, across_too, beside)


def on_device(dens, upsample, src_geom, targ, lists, lens):
    groups = lax.axis_size("patch")
    geom = jnp.transpose(src_geom, (1, 0, 2))
    gathered = lax.all_to_all(spread(dens), "helper", 0, 0, tiled=True).reshape(256, NODES, LANES)
    head, src, targ, ups, table = coefficients_head(lists, lens, targ, upsample.T, geom)
    gathered, head = lax.optimization_barrier((gathered, head))
    odd = lax.axis_index("patch").astype(jnp.int32) & 1
    near_edge = lax.dynamic_slice_in_dim(gathered, 192 - 192 * odd, 64)
    over = [(g, (g + 2 * (g % 2) - 1) % groups) for g in range(groups)]
    across = lax.ppermute(lax.dynamic_slice_in_dim(gathered, 192 * odd, 32), "patch", over)
    across_too = lax.ppermute(lax.dynamic_slice_in_dim(gathered, 192 * odd + 32, 32), "patch", over)
    beside = lax.ppermute(near_edge, "patch", [(g, g ^ 1) for g in range(groups)])
    tail = coefficients_tail(table, src, targ, ups)
    return combine(lists, head, tail, gathered, across, across_too, beside)


def solution(mesh):
    in_specs = (
        P(("patch", "helper"), None, None),
        P(),
        P("patch", None, None),
        P(None, ("patch", "helper")),
        P(("patch", "helper"), None),
        P(("patch", "helper")),
    )
    out_specs = P(("patch", "helper"), None)
    return jax.shard_map(on_device, mesh=mesh, in_specs=in_specs, out_specs=out_specs, check_vma=False)
```

```python
import functools
import math

import jax
import jax.numpy as jnp
from jax import lax
from jax.experimental import pallas as pl
from jax.experimental.pallas import tpu as pltpu
from jax.sharding import PartitionSpec as P

CHECKS = 16
NODES = 16
SLOTS = 16
LANES = 128
F32 = jnp.float32
BF16 = jnp.bfloat16

LN2 = math.log(2.0)
KAPPA = 2.0 / LN2
REACH = 0.5

LEFT = (0, 0, 1, 1, 0, 2)
RIGHT = (0, 1, 0, 1, 2, 0)
DEPTH = 64
TAIL = 16
VMEM_ALL = 67043328
VMEM_KEPT = 24 << 20


def angle(m):
    return 2.0 * math.pi * m / CHECKS


def log_weight(m):
    weight = 0.75 / (CHECKS * (1.25 + math.cos(angle(m))))
    return math.log2(weight * KAPPA / (4.0 * math.pi))


def halves(x):
    high = x.astype(BF16)
    return high, (x - high.astype(F32)).astype(BF16)


def thirds(x):
    high = x.astype(BF16).astype(F32)
    rest = x - high
    middle = rest.astype(BF16).astype(F32)
    return high, middle, rest - middle


def stacked(features, order):
    parts = thirds(features)
    rows = [parts[i] for i in order]
    rows.append(jnp.zeros((DEPTH - 8 * len(order), LANES), F32))
    return jnp.concatenate(rows, axis=0)


def total_of(x):
    return jnp.sum(x, axis=0, keepdims=True)


def circle(targ, b):
    t = targ[:, pl.ds(pl.multiple_of(b * LANES, LANES), LANES)]
    radius = t[9:10] * KAPPA
    return t[0:3] * KAPPA, radius * t[3:6], 2 * radius * t[3:6], 2 * radius * t[6:9]


def collect(lists, lens, targ_in, ups_in, geom, src, targ, ups, table, sem, sem_panel):
    small = [pltpu.make_async_copy(targ_in, targ, sem.at[0]), pltpu.make_async_copy(ups_in, ups, sem.at[1])]
    for copy in small:
        copy.start()

    def fetch(at):
        panel = geom.at[:, lists[at >> 4, at & 15]]
        return pltpu.make_async_copy(panel, src.at[at, pl.ds(0, 7)], sem_panel.at[at])

    items = jnp.int32(0)
    for b in range(4):

        def row(l, i, b=b):
            table[i] = SLOTS * b + l
            fetch(SLOTS * b + l).start()
            return i + 1

        items = lax.fori_loop(0, lens[b], row, items)
    table[4 * SLOTS] = items
    for copy in small:
        copy.wait()

    def arrived(i, carry):
        fetch(table[i]).wait()
        return carry

    return lambda: lax.fori_loop(0, items, arrived, 0)


def head_body(lists, lens, targ_in, ups_in, geom, out, src, targ, ups, table, *scratch):
    *scratch, sem, sem_panel = scratch
    wait = collect(lists, lens, targ_in, ups_in, geom, src, targ, ups, table, sem, sem_panel)
    coefficients_body(table, src, targ, ups, out, *scratch, tail=False, wait=wait)


def tail_body(table, src, targ, ups, out, *scratch):
    coefficients_body(table, src, targ, ups, out, *scratch, tail=True, wait=None)


def coefficients_body(table, src, targ, ups, out, wts, org, lhs, tile, pairs, far, *, tail, wait):
    every = table[4 * SLOTS]
    late = jnp.minimum(every >> 1, TAIL)
    first, items = (every - late, late) if tail else (0, every - late)

    def entry(i):
        return table[first + jnp.minimum(i, items - 1)]

    out[...] = jnp.zeros_like(out)
    zero = jnp.zeros((1, LANES), F32)
    one = jnp.ones((1, LANES), F32)
    far[...] = jnp.zeros_like(far)

    def build(b, carry):
        position, lift, normal, tangent = circle(targ, b)
        origin = jnp.broadcast_to(jnp.mean(position, axis=1, keepdims=True), (3, LANES))
        org[b, 0:3] = origin
        center = position - origin + lift
        for m in range(CHECKS):
            point = center + math.cos(angle(m)) * normal + math.sin(angle(m)) * tangent
            square = total_of(point * point)
            far[0:1] = jnp.maximum(far[0:1], square)
            features = jnp.concatenate([square, point, one, zero, zero, zero], axis=0)
            wts[b, :, m * LANES : (m + 1) * LANES] = stacked(features, LEFT).astype(BF16)
        return carry

    lax.fori_loop(entry(0) >> 4, (entry(items - 1) >> 4) + 1, build, 0)
    if wait:
        wait()

    def prepare(i, slot):
        at = entry(i)
        g = src[at, 0:7]
        y = g[0:3] * KAPPA - org[at >> 4, 0:3]
        n = g[3:6] * KAPPA
        square = total_of(y * y)
        far[1:2] = jnp.maximum(far[1:2], square)
        for_square = jnp.concatenate([one, -2.0 * y, square, zero, zero, zero], axis=0)
        for_facing = jnp.concatenate([zero, n, -total_of(n * y), zero, zero, zero], axis=0)
        both = jnp.concatenate([stacked(for_square, RIGHT), stacked(for_facing, RIGHT)], axis=0)
        both = both.T.astype(BF16)
        for j in range(8):
            lhs[slot, 32 * j : 32 * j + 16] = both[16 * j : 16 * j + 16, 0:DEPTH]
            lhs[slot, 32 * j + 16 : 32 * j + 32] = both[16 * j : 16 * j + 16, DEPTH : 2 * DEPTH]

    def two_points(b, slot, k):
        return jnp.dot(lhs[slot], wts[b, :, 256 * k : 256 * k + 256], preferred_element_type=F32)

    def flush(i):
        at = entry(i)
        high, low = halves(ups[...] * src[at, 6:7])
        tile_high, tile_low = halves(tile[...])
        left = jnp.concatenate(
            [
                jnp.concatenate([high, high], axis=1),
                jnp.concatenate([low, jnp.zeros_like(low)], axis=1),
            ],
            axis=0,
        )
        right = jnp.concatenate([tile_high, tile_low], axis=0)
        sums = jnp.dot(left, right, preferred_element_type=F32)
        rows = pl.ds(pl.multiple_of((at & 15) * NODES, NODES), NODES)
        out[at >> 4, rows] = sums[0:NODES] + sums[NODES : 2 * NODES]

    def potential(square, facing, m):
        inverse = lax.rsqrt(square)
        single = jnp.exp2(log_weight(m) - square * inverse) * inverse
        return single + single * (inverse * (inverse + LN2) * facing)

    def step(i, slot):
        flush(jnp.maximum(i - 1, 0))
        next_b = entry(i + 1) >> 4
        sums = [None] * 8
        for k in range(CHECKS // 2):
            r = pairs[:, 256 * k : 256 * k + 256]
            for half in range(2):
                cols = slice(LANES * half, LANES * half + LANES)
                for x in range(8):
                    value = potential(r[32 * x : 32 * x + 16, cols], r[32 * x + 16 : 32 * x + 32, cols], 2 * k + half)
                    sums[x] = value if sums[x] is None else sums[x] + value
            pairs[:, 256 * k : 256 * k + 256] = two_points(next_b, 1 - slot, k)
        for x in range(8):
            tile[16 * x : 16 * x + 16] = sums[x]
        prepare(i + 2, slot)

    tile[...] = jnp.zeros_like(tile)
    for i in range(2):
        prepare(i, i)
    for k in range(CHECKS // 2):
        pairs[:, 256 * k : 256 * k + 256] = two_points(entry(0) >> 4, 0, k)

    def steps(i, carry):
        for j in range(2):
            step(2 * i + j, j)
        return carry

    lax.fori_loop(0, (items + 1) >> 1, steps, 0)
    flush(items - 1)

    @pl.when(jnp.max(far[...]) > REACH * KAPPA * KAPPA)
    def _():
        def slow(i, carry):
            at = entry(i)
            columns = jnp.concatenate([src[at, 0:7], zero], axis=0).T
            y = [columns[:, a : a + 1] * KAPPA for a in range(3)]
            n = [columns[:, a + 3 : a + 4] * KAPPA for a in range(3)]
            position, lift, normal, tangent = circle(targ, at >> 4)
            center = position + lift
            tile[...] = jnp.zeros_like(tile)
            for m in range(CHECKS):
                point = center + math.cos(angle(m)) * normal + math.sin(angle(m)) * tangent
                for x in range(8):
                    rows = slice(16 * x, 16 * x + 16)
                    d = [point[a : a + 1] - y[a][rows] for a in range(3)]
                    square = d[0] * d[0] + d[1] * d[1] + d[2] * d[2]
                    facing = d[0] * n[0][rows] + d[1] * n[1][rows] + d[2] * n[2][rows]
                    tile[rows] += potential(square, facing, m)
            flush(i)
            return carry

        lax.fori_loop(0, items, slow, 0)


VMEM = pl.BlockSpec(memory_space=pltpu.VMEM)
KEPT = pl.BlockSpec(memory_space=pl.ANY)
WORK = [
    pltpu.VMEM((4, DEPTH, CHECKS * LANES), BF16),
    pltpu.VMEM((4, 8, LANES), F32),
    pltpu.VMEM((2, 2 * LANES, DEPTH), BF16),
    pltpu.VMEM((LANES, LANES), F32),
    pltpu.VMEM((2 * LANES, CHECKS * LANES), F32),
    pltpu.VMEM((8, LANES), F32),
]
SUMS = pltpu.VMEM((4, SLOTS * NODES, LANES), F32)


def cost(items):
    points = items * 128 * 128 * CHECKS
    return pl.CostEstimate(flops=40 * points, bytes_accessed=2 << 20, transcendentals=2 * points)


def coefficients_head(lists, lens, targ, ups, geom):
    return pl.pallas_call(
        head_body,
        grid_spec=pltpu.PrefetchScalarGridSpec(
            num_scalar_prefetch=2,
            grid=(1,),
            in_specs=[KEPT] * 3,
            out_specs=[VMEM] * 4 + [pl.BlockSpec(memory_space=pltpu.SMEM)],
            scratch_shapes=WORK + [pltpu.SemaphoreType.DMA((2,)), pltpu.SemaphoreType.DMA((4 * SLOTS,))],
        ),
        out_shape=[
            SUMS,
            pltpu.VMEM((4 * SLOTS, 8, LANES), F32),
            pltpu.VMEM(targ.shape, F32),
            pltpu.VMEM(ups.shape, F32),
            jax.ShapeDtypeStruct((4 * SLOTS + 1,), jnp.int32),
        ],
        cost_estimate=cost(60 - TAIL),
        compiler_params=pltpu.CompilerParams(vmem_limit_bytes=VMEM_ALL - 3800000),
        name="coefficients_head",
    )(lists, lens, targ, ups, geom)


def coefficients_tail(table, src, targ, ups):
    return pl.pallas_call(
        tail_body,
        grid_spec=pltpu.PrefetchScalarGridSpec(
            num_scalar_prefetch=1, grid=(1,), in_specs=[VMEM] * 3, out_specs=VMEM, scratch_shapes=WORK
        ),
        out_shape=SUMS,
        cost_estimate=cost(TAIL),
        compiler_params=pltpu.CompilerParams(vmem_limit_bytes=VMEM_KEPT),
        name="coefficients_tail",
    )(table, src, targ, ups)


def combine_body(lists, head, tail, own, across, beside, out, kept, sem):
    side = 1 - 2 * (lax.axis_index("patch") & 1)

    def nodes(e):
        which = ((e - 64) >> 8) * side
        edge = jnp.where(which < 0, across[e & 63], beside[e & 63])
        return jnp.where(which == 0, own[(e - 64) & 255], edge)

    stores = []
    for b in range(4):
        high, low = halves(jnp.concatenate([nodes(lists[b, l]) for l in range(SLOTS)], axis=0))
        c_high, c_low = halves((head[b] + tail[b]).T)
        value = jnp.dot(c_high, high, preferred_element_type=F32)
        value += jnp.dot(c_high, low, preferred_element_type=F32)
        value += jnp.dot(c_low, high, preferred_element_type=F32)
        kept[b] = value
        stores.append(pltpu.make_async_copy(kept.at[b], out.at[pl.ds(b * LANES, LANES)], sem.at[b]))
        stores[b].start()
    for store in stores:
        store.wait()


def combine(lists, head, tail, own, across, beside):
    return pl.pallas_call(
        combine_body,
        grid_spec=pltpu.PrefetchScalarGridSpec(
            num_scalar_prefetch=1,
            grid=(1,),
            in_specs=[VMEM] * 5,
            out_specs=KEPT,
            scratch_shapes=[pltpu.VMEM((4, LANES, LANES), F32), pltpu.SemaphoreType.DMA((4,))],
        ),
        out_shape=jax.ShapeDtypeStruct((4 * LANES, LANES), F32),
        cost_estimate=pl.CostEstimate(flops=4 << 24, bytes_accessed=4 << 20, transcendentals=0),
        compiler_params=pltpu.CompilerParams(vmem_limit_bytes=24 << 20),
        name="combine",
    )(lists, head, tail, own, across, beside)


def on_device(dens, upsample, src_geom, targ, lists, lens):
    groups = lax.axis_size("patch")
    geom = jnp.transpose(src_geom, (1, 0, 2))
    gathered = lax.all_gather(dens, "helper", axis=0, tiled=True)
    head, src, targ, ups, table = coefficients_head(lists, lens, targ, upsample.T, geom)
    gathered, head = lax.optimization_barrier((gathered, head))
    odd = lax.axis_index("patch").astype(jnp.int32) & 1
    far_edge = lax.dynamic_slice_in_dim(gathered, 192 * odd, 64)
    near_edge = lax.dynamic_slice_in_dim(gathered, 192 - 192 * odd, 64)
    across = lax.ppermute(far_edge, "patch", [(g, (g + 2 * (g % 2) - 1) % groups) for g in range(groups)])
    beside = lax.ppermute(near_edge, "patch", [(g, g ^ 1) for g in range(groups)])
    tail = coefficients_tail(table, src, targ, ups)
    return combine(lists, head, tail, gathered, across, beside)


def solution(mesh):
    in_specs = (
        P(("patch", "helper"), None, None),
        P(),
        P("patch", None, None),
        P(None, ("patch", "helper")),
        P(("patch", "helper"), None),
        P(("patch", "helper")),
    )
    out_specs = P(("patch", "helper"), None)
    return jax.shard_map(on_device, mesh=mesh, in_specs=in_specs, out_specs=out_specs, check_vma=False)
```

```python
import functools
import math

import jax
import jax.numpy as jnp
from jax import lax
from jax.experimental import pallas as pl
from jax.experimental.pallas import tpu as pltpu
from jax.sharding import PartitionSpec as P

CHECKS = 16
NODES = 16
SLOTS = 16
LANES = 128
F32 = jnp.float32
BF16 = jnp.bfloat16

LN2 = math.log(2.0)
KAPPA = 2.0 / LN2
REACH = 0.5

LEFT = (0, 0, 1, 1, 0, 2)
RIGHT = (0, 1, 0, 1, 2, 0)
DEPTH = 64
TAIL = 16
ORDER = [0, 1, 5, 4, 3, 2, 6, 7]
VMEM_ALL = 67043328
VMEM_KEPT = 24 << 20


def angle(m):
    return 2.0 * math.pi * m / CHECKS


def log_weight(m):
    weight = 0.75 / (CHECKS * (1.25 + math.cos(angle(m))))
    return math.log2(weight * KAPPA / (4.0 * math.pi))


def halves(x):
    high = x.astype(BF16)
    return high, (x - high.astype(F32)).astype(BF16)


def thirds(x):
    high = x.astype(BF16).astype(F32)
    rest = x - high
    middle = rest.astype(BF16).astype(F32)
    return high, middle, rest - middle


def stacked(features, order):
    parts = thirds(features)
    rows = [parts[i] for i in order]
    rows.append(jnp.zeros((DEPTH - 8 * len(order), LANES), F32))
    return jnp.concatenate(rows, axis=0)


def total_of(x):
    return jnp.sum(x, axis=0, keepdims=True)


def circle(targ, b):
    t = targ[:, pl.ds(pl.multiple_of(b * LANES, LANES), LANES)]
    radius = t[9:10] * KAPPA
    return t[0:3] * KAPPA, radius * t[3:6], 2 * radius * t[3:6], 2 * radius * t[6:9]


def spread_body(x, out, sem):
    copies = [pltpu.make_async_copy(x, out.at[k], sem.at[k]) for k in range(8)]
    for copy in copies:
        copy.start()
    for copy in copies:
        copy.wait()


def spread(x):
    return pl.pallas_call(
        spread_body,
        in_specs=[pl.BlockSpec(memory_space=pltpu.VMEM)],
        out_specs=pl.BlockSpec(memory_space=pl.ANY),
        out_shape=jax.ShapeDtypeStruct((8, *x.shape), F32),
        scratch_shapes=[pltpu.SemaphoreType.DMA((8,))],
        name="spread",
    )(x)


def collect(lists, lens, targ_in, ups_in, geom, src, targ, ups, table, sem, sem_panel):
    small = [pltpu.make_async_copy(targ_in, targ, sem.at[0]), pltpu.make_async_copy(ups_in, ups, sem.at[1])]
    for copy in small:
        copy.start()

    def fetch(at):
        panel = geom.at[:, lists[at >> 4, at & 15]]
        return pltpu.make_async_copy(panel, src.at[at, pl.ds(0, 7)], sem_panel.at[at])

    items = jnp.int32(0)
    for b in range(4):

        def row(l, i, b=b):
            table[i] = SLOTS * b + l
            fetch(SLOTS * b + l).start()
            return i + 1

        items = lax.fori_loop(0, lens[b], row, items)
    table[4 * SLOTS] = items
    for copy in small:
        copy.wait()

    def arrived(i, carry):
        fetch(table[i]).wait()
        return carry

    return lambda: lax.fori_loop(0, items, arrived, 0)


def head_body(lists, lens, targ_in, ups_in, geom, out, src, targ, ups, table, *scratch):
    *scratch, sem, sem_panel = scratch
    wait = collect(lists, lens, targ_in, ups_in, geom, src, targ, ups, table, sem, sem_panel)
    coefficients_body(table, src, targ, ups, out, *scratch, tail=False, wait=wait)


def tail_body(table, src, targ, ups, out, *scratch):
    coefficients_body(table, src, targ, ups, out, *scratch, tail=True, wait=None)


def coefficients_body(table, src, targ, ups, out, wts, org, lhs, tile, pairs, far, *, tail, wait):
    every = table[4 * SLOTS]
    late = jnp.minimum(every >> 1, TAIL)
    first, items = (every - late, late) if tail else (0, every - late)

    def entry(i):
        return table[first + jnp.minimum(i, items - 1)]

    out[...] = jnp.zeros_like(out)
    zero = jnp.zeros((1, LANES), F32)
    one = jnp.ones((1, LANES), F32)
    far[...] = jnp.zeros_like(far)

    def build(b, carry):
        position, lift, normal, tangent = circle(targ, b)
        origin = jnp.broadcast_to(jnp.mean(position, axis=1, keepdims=True), (3, LANES))
        org[b, 0:3] = origin
        center = position - origin + lift
        for m in range(CHECKS):
            point = center + math.cos(angle(m)) * normal + math.sin(angle(m)) * tangent
            square = total_of(point * point)
            far[0:1] = jnp.maximum(far[0:1], square)
            features = jnp.concatenate([square, point, one, zero, zero, zero], axis=0)
            wts[b, :, m * LANES : (m + 1) * LANES] = stacked(features, LEFT).astype(BF16)
        return carry

    lax.fori_loop(entry(0) >> 4, (entry(items - 1) >> 4) + 1, build, 0)
    if wait:
        wait()

    def prepare(i, slot):
        at = entry(i)
        g = src[at, 0:7]
        y = g[0:3] * KAPPA - org[at >> 4, 0:3]
        n = g[3:6] * KAPPA
        square = total_of(y * y)
        far[1:2] = jnp.maximum(far[1:2], square)
        for_square = jnp.concatenate([one, -2.0 * y, square, zero, zero, zero], axis=0)
        for_facing = jnp.concatenate([zero, n, -total_of(n * y), zero, zero, zero], axis=0)
        both = jnp.concatenate([stacked(for_square, RIGHT), stacked(for_facing, RIGHT)], axis=0)
        both = both.T.astype(BF16)
        for j in range(8):
            lhs[slot, 32 * j : 32 * j + 16] = both[16 * j : 16 * j + 16, 0:DEPTH]
            lhs[slot, 32 * j + 16 : 32 * j + 32] = both[16 * j : 16 * j + 16, DEPTH : 2 * DEPTH]

    def two_points(b, slot, k):
        return jnp.dot(lhs[slot], wts[b, :, 256 * k : 256 * k + 256], preferred_element_type=F32)

    def flush(i):
        at = entry(i)
        high, low = halves(ups[...] * src[at, 6:7])
        tile_high, tile_low = halves(tile[...])
        left = jnp.concatenate(
            [
                jnp.concatenate([high, high], axis=1),
                jnp.concatenate([low, jnp.zeros_like(low)], axis=1),
            ],
            axis=0,
        )
        right = jnp.concatenate([tile_high, tile_low], axis=0)
        sums = jnp.dot(left, right, preferred_element_type=F32)
        rows = pl.ds(pl.multiple_of((at & 15) * NODES, NODES), NODES)
        out[at >> 4, rows] = sums[0:NODES] + sums[NODES : 2 * NODES]

    def potential(square, facing, m):
        inverse = lax.rsqrt(square)
        single = jnp.exp2(log_weight(m) - square * inverse) * inverse
        return single + single * (inverse * (inverse + LN2) * facing)

    def step(i, slot):
        flush(jnp.maximum(i - 1, 0))
        next_b = entry(i + 1) >> 4
        sums = [None] * 8
        for k in range(CHECKS // 2):
            r = pairs[:, 256 * k : 256 * k + 256]
            for half in range(2):
                cols = slice(LANES * half, LANES * half + LANES)
                for x in range(8):
                    value = potential(r[32 * x : 32 * x + 16, cols], r[32 * x + 16 : 32 * x + 32, cols], 2 * k + half)
                    sums[x] = value if sums[x] is None else sums[x] + value
            pairs[:, 256 * k : 256 * k + 256] = two_points(next_b, 1 - slot, k)
        for x in range(8):
            tile[16 * x : 16 * x + 16] = sums[x]
        prepare(i + 2, slot)

    tile[...] = jnp.zeros_like(tile)
    for i in range(2):
        prepare(i, i)
    for k in range(CHECKS // 2):
        pairs[:, 256 * k : 256 * k + 256] = two_points(entry(0) >> 4, 0, k)

    def steps(i, carry):
        for j in range(2):
            step(2 * i + j, j)
        return carry

    lax.fori_loop(0, (items + 1) >> 1, steps, 0)
    flush(items - 1)

    @pl.when(jnp.max(far[...]) > REACH * KAPPA * KAPPA)
    def _():
        def slow(i, carry):
            at = entry(i)
            columns = jnp.concatenate([src[at, 0:7], zero], axis=0).T
            y = [columns[:, a : a + 1] * KAPPA for a in range(3)]
            n = [columns[:, a + 3 : a + 4] * KAPPA for a in range(3)]
            position, lift, normal, tangent = circle(targ, at >> 4)
            center = position + lift
            tile[...] = jnp.zeros_like(tile)
            for m in range(CHECKS):
                point = center + math.cos(angle(m)) * normal + math.sin(angle(m)) * tangent
                for x in range(8):
                    rows = slice(16 * x, 16 * x + 16)
                    d = [point[a : a + 1] - y[a][rows] for a in range(3)]
                    square = d[0] * d[0] + d[1] * d[1] + d[2] * d[2]
                    facing = d[0] * n[0][rows] + d[1] * n[1][rows] + d[2] * n[2][rows]
                    tile[rows] += potential(square, facing, m)
            flush(i)
            return carry

        lax.fori_loop(0, items, slow, 0)


VMEM = pl.BlockSpec(memory_space=pltpu.VMEM)
KEPT = pl.BlockSpec(memory_space=pl.ANY)
WORK = [
    pltpu.VMEM((4, DEPTH, CHECKS * LANES), BF16),
    pltpu.VMEM((4, 8, LANES), F32),
    pltpu.VMEM((2, 2 * LANES, DEPTH), BF16),
    pltpu.VMEM((LANES, LANES), F32),
    pltpu.VMEM((2 * LANES, CHECKS * LANES), F32),
    pltpu.VMEM((8, LANES), F32),
]
SUMS = pltpu.VMEM((4, SLOTS * NODES, LANES), F32)


def cost(items):
    points = items * 128 * 128 * CHECKS
    return pl.CostEstimate(flops=40 * points, bytes_accessed=2 << 20, transcendentals=2 * points)


def coefficients_head(lists, lens, targ, ups, geom):
    return pl.pallas_call(
        head_body,
        grid_spec=pltpu.PrefetchScalarGridSpec(
            num_scalar_prefetch=2,
            grid=(1,),
            in_specs=[KEPT] * 3,
            out_specs=[VMEM] * 4 + [pl.BlockSpec(memory_space=pltpu.SMEM)],
            scratch_shapes=WORK + [pltpu.SemaphoreType.DMA((2,)), pltpu.SemaphoreType.DMA((4 * SLOTS,))],
        ),
        out_shape=[
            SUMS,
            pltpu.VMEM((4 * SLOTS, 8, LANES), F32),
            pltpu.VMEM(targ.shape, F32),
            pltpu.VMEM(ups.shape, F32),
            jax.ShapeDtypeStruct((4 * SLOTS + 1,), jnp.int32),
        ],
        cost_estimate=cost(60 - TAIL),
        compiler_params=pltpu.CompilerParams(vmem_limit_bytes=VMEM_ALL - 3800000),
        name="coefficients_head",
    )(lists, lens, targ, ups, geom)


def coefficients_tail(table, src, targ, ups):
    return pl.pallas_call(
        tail_body,
        grid_spec=pltpu.PrefetchScalarGridSpec(
            num_scalar_prefetch=1, grid=(1,), in_specs=[VMEM] * 3, out_specs=VMEM, scratch_shapes=WORK
        ),
        out_shape=SUMS,
        cost_estimate=cost(TAIL),
        compiler_params=pltpu.CompilerParams(vmem_limit_bytes=VMEM_KEPT),
        name="coefficients_tail",
    )(table, src, targ, ups)


def combine_body(lists, head, tail, own, across, beside, out, kept, sem):
    side = 1 - 2 * (lax.axis_index("patch") & 1)

    def nodes(e):
        which = ((e - 64) >> 8) * side
        edge = jnp.where(which < 0, across[e & 63], beside[e & 63])
        panel = (e - 64) & 255
        owner = panel >> 5
        owner = jnp.where((owner >= 2) & (owner < 6), 7 - owner, owner)
        return jnp.where(which == 0, own[32 * owner + (panel & 31)], edge)

    stores = []
    for b in range(4):
        high, low = halves(jnp.concatenate([nodes(lists[b, l]) for l in range(SLOTS)], axis=0))
        c_high, c_low = halves((head[b] + tail[b]).T)
        value = jnp.dot(c_high, high, preferred_element_type=F32)
        value += jnp.dot(c_high, low, preferred_element_type=F32)
        value += jnp.dot(c_low, high, preferred_element_type=F32)
        kept[b] = value
        stores.append(pltpu.make_async_copy(kept.at[b], out.at[pl.ds(b * LANES, LANES)], sem.at[b]))
        stores[b].start()
    for store in stores:
        store.wait()


def combine(lists, head, tail, own, across, beside):
    return pl.pallas_call(
        combine_body,
        grid_spec=pltpu.PrefetchScalarGridSpec(
            num_scalar_prefetch=1,
            grid=(1,),
            in_specs=[VMEM] * 5,
            out_specs=KEPT,
            scratch_shapes=[pltpu.VMEM((4, LANES, LANES), F32), pltpu.SemaphoreType.DMA((4,))],
        ),
        out_shape=jax.ShapeDtypeStruct((4 * LANES, LANES), F32),
        cost_estimate=pl.CostEstimate(flops=4 << 24, bytes_accessed=4 << 20, transcendentals=0),
        compiler_params=pltpu.CompilerParams(vmem_limit_bytes=24 << 20),
        name="combine",
    )(lists, head, tail, own, across, beside)


def on_device(dens, upsample, src_geom, targ, lists, lens):
    groups = lax.axis_size("patch")
    geom = jnp.transpose(src_geom, (1, 0, 2))
    gathered = lax.all_to_all(spread(dens), "helper", 0, 0, axis_index_groups=[ORDER], tiled=True).reshape(256, NODES, LANES)
    head, src, targ, ups, table = coefficients_head(lists, lens, targ, upsample.T, geom)
    gathered, head = lax.optimization_barrier((gathered, head))
    odd = lax.axis_index("patch").astype(jnp.int32) & 1
    far_edge = lax.dynamic_slice_in_dim(gathered, 192 * odd, 64)
    near_edge = lax.dynamic_slice_in_dim(gathered, 192 - 192 * odd, 64)
    across = lax.ppermute(far_edge, "patch", [(g, (g + 2 * (g % 2) - 1) % groups) for g in range(groups)])
    beside = lax.ppermute(near_edge, "patch", [(g, g ^ 1) for g in range(groups)])
    tail = coefficients_tail(table, src, targ, ups)
    return combine(lists, head, tail, gathered, across, beside)


def solution(mesh):
    in_specs = (
        P(("patch", "helper"), None, None),
        P(),
        P("patch", None, None),
        P(None, ("patch", "helper")),
        P(("patch", "helper"), None),
        P(("patch", "helper")),
    )
    out_specs = P(("patch", "helper"), None)
    return jax.shard_map(on_device, mesh=mesh, in_specs=in_specs, out_specs=out_specs, check_vma=False)
```

```python
import functools
import math

import jax
import jax.numpy as jnp
from jax import lax
from jax.experimental import pallas as pl
from jax.experimental.pallas import tpu as pltpu
from jax.sharding import PartitionSpec as P

CHECKS = 16
NODES = 16
SLOTS = 16
LANES = 128
F32 = jnp.float32
BF16 = jnp.bfloat16

LN2 = math.log(2.0)
KAPPA = 2.0 / LN2
REACH = 0.5

LEFT = (0, 0, 1, 1, 0, 2)
RIGHT = (0, 1, 0, 1, 2, 0)
DEPTH = 64
TAIL = 16
ORDER = [0, 1, 2, 3, 5, 6, 7, 4]
VMEM_ALL = 67043328
VMEM_KEPT = 24 << 20


def angle(m):
    return 2.0 * math.pi * m / CHECKS


def log_weight(m):
    weight = 0.75 / (CHECKS * (1.25 + math.cos(angle(m))))
    return math.log2(weight * KAPPA / (4.0 * math.pi))


def halves(x):
    high = x.astype(BF16)
    return high, (x - high.astype(F32)).astype(BF16)


def thirds(x):
    high = x.astype(BF16).astype(F32)
    rest = x - high
    middle = rest.astype(BF16).astype(F32)
    return high, middle, rest - middle


def stacked(features, order):
    parts = thirds(features)
    rows = [parts[i] for i in order]
    rows.append(jnp.zeros((DEPTH - 8 * len(order), LANES), F32))
    return jnp.concatenate(rows, axis=0)


def total_of(x):
    return jnp.sum(x, axis=0, keepdims=True)


def circle(targ, b):
    t = targ[:, pl.ds(pl.multiple_of(b * LANES, LANES), LANES)]
    radius = t[9:10] * KAPPA
    return t[0:3] * KAPPA, radius * t[3:6], 2 * radius * t[3:6], 2 * radius * t[6:9]


def spread_body(x, out, sem):
    copies = [pltpu.make_async_copy(x, out.at[k], sem.at[k]) for k in range(8)]
    for copy in copies:
        copy.start()
    for copy in copies:
        copy.wait()


def spread(x):
    return pl.pallas_call(
        spread_body,
        in_specs=[pl.BlockSpec(memory_space=pltpu.VMEM)],
        out_specs=pl.BlockSpec(memory_space=pl.ANY),
        out_shape=jax.ShapeDtypeStruct((8, *x.shape), F32),
        scratch_shapes=[pltpu.SemaphoreType.DMA((8,))],
        name="spread",
    )(x)


def collect(lists, lens, targ_in, ups_in, geom, src, targ, ups, table, sem, sem_panel):
    small = [pltpu.make_async_copy(targ_in, targ, sem.at[0]), pltpu.make_async_copy(ups_in, ups, sem.at[1])]
    for copy in small:
        copy.start()

    def fetch(at):
        panel = geom.at[:, lists[at >> 4, at & 15]]
        return pltpu.make_async_copy(panel, src.at[at, pl.ds(0, 7)], sem_panel.at[at])

    items = jnp.int32(0)
    for b in range(4):

        def row(l, i, b=b):
            table[i] = SLOTS * b + l
            fetch(SLOTS * b + l).start()
            return i + 1

        items = lax.fori_loop(0, lens[b], row, items)
    table[4 * SLOTS] = items
    for copy in small:
        copy.wait()

    def arrived(i, carry):
        fetch(table[i]).wait()
        return carry

    return lambda: lax.fori_loop(0, items, arrived, 0)


def head_body(lists, lens, targ_in, ups_in, geom, out, src, targ, ups, table, *scratch):
    *scratch, sem, sem_panel = scratch
    wait = collect(lists, lens, targ_in, ups_in, geom, src, targ, ups, table, sem, sem_panel)
    coefficients_body(table, src, targ, ups, out, *scratch, tail=False, wait=wait)


def tail_body(table, src, targ, ups, out, *scratch):
    coefficients_body(table, src, targ, ups, out, *scratch, tail=True, wait=None)


def coefficients_body(table, src, targ, ups, out, wts, org, lhs, tile, pairs, far, *, tail, wait):
    every = table[4 * SLOTS]
    late = jnp.minimum(every >> 1, TAIL)
    first, items = (every - late, late) if tail else (0, every - late)

    def entry(i):
        return table[first + jnp.minimum(i, items - 1)]

    out[...] = jnp.zeros_like(out)
    zero = jnp.zeros((1, LANES), F32)
    one = jnp.ones((1, LANES), F32)
    far[...] = jnp.zeros_like(far)

    def build(b, carry):
        position, lift, normal, tangent = circle(targ, b)
        origin = jnp.broadcast_to(jnp.mean(position, axis=1, keepdims=True), (3, LANES))
        org[b, 0:3] = origin
        center = position - origin + lift
        for m in range(CHECKS):
            point = center + math.cos(angle(m)) * normal + math.sin(angle(m)) * tangent
            square = total_of(point * point)
            far[0:1] = jnp.maximum(far[0:1], square)
            features = jnp.concatenate([square, point, one, zero, zero, zero], axis=0)
            wts[b, :, m * LANES : (m + 1) * LANES] = stacked(features, LEFT).astype(BF16)
        return carry

    lax.fori_loop(entry(0) >> 4, (entry(items - 1) >> 4) + 1, build, 0)
    if wait:
        wait()

    def prepare(i, slot):
        at = entry(i)
        g = src[at, 0:7]
        y = g[0:3] * KAPPA - org[at >> 4, 0:3]
        n = g[3:6] * KAPPA
        square = total_of(y * y)
        far[1:2] = jnp.maximum(far[1:2], square)
        for_square = jnp.concatenate([one, -2.0 * y, square, zero, zero, zero], axis=0)
        for_facing = jnp.concatenate([zero, n, -total_of(n * y), zero, zero, zero], axis=0)
        both = jnp.concatenate([stacked(for_square, RIGHT), stacked(for_facing, RIGHT)], axis=0)
        both = both.T.astype(BF16)
        for j in range(8):
            lhs[slot, 32 * j : 32 * j + 16] = both[16 * j : 16 * j + 16, 0:DEPTH]
            lhs[slot, 32 * j + 16 : 32 * j + 32] = both[16 * j : 16 * j + 16, DEPTH : 2 * DEPTH]

    def two_points(b, slot, k):
        return jnp.dot(lhs[slot], wts[b, :, 256 * k : 256 * k + 256], preferred_element_type=F32)

    def flush(i):
        at = entry(i)
        high, low = halves(ups[...] * src[at, 6:7])
        tile_high, tile_low = halves(tile[...])
        left = jnp.concatenate(
            [
                jnp.concatenate([high, high], axis=1),
                jnp.concatenate([low, jnp.zeros_like(low)], axis=1),
            ],
            axis=0,
        )
        right = jnp.concatenate([tile_high, tile_low], axis=0)
        sums = jnp.dot(left, right, preferred_element_type=F32)
        rows = pl.ds(pl.multiple_of((at & 15) * NODES, NODES), NODES)
        out[at >> 4, rows] = sums[0:NODES] + sums[NODES : 2 * NODES]

    def potential(square, facing, m):
        inverse = lax.rsqrt(square)
        single = jnp.exp2(log_weight(m) - square * inverse) * inverse
        return single + single * (inverse * (inverse + LN2) * facing)

    def step(i, slot):
        flush(jnp.maximum(i - 1, 0))
        next_b = entry(i + 1) >> 4
        sums = [None] * 8
        for k in range(CHECKS // 2):
            r = pairs[:, 256 * k : 256 * k + 256]
            for half in range(2):
                cols = slice(LANES * half, LANES * half + LANES)
                for x in range(8):
                    value = potential(r[32 * x : 32 * x + 16, cols], r[32 * x + 16 : 32 * x + 32, cols], 2 * k + half)
                    sums[x] = value if sums[x] is None else sums[x] + value
            pairs[:, 256 * k : 256 * k + 256] = two_points(next_b, 1 - slot, k)
        for x in range(8):
            tile[16 * x : 16 * x + 16] = sums[x]
        prepare(i + 2, slot)

    tile[...] = jnp.zeros_like(tile)
    for i in range(2):
        prepare(i, i)
    for k in range(CHECKS // 2):
        pairs[:, 256 * k : 256 * k + 256] = two_points(entry(0) >> 4, 0, k)

    def steps(i, carry):
        for j in range(2):
            step(2 * i + j, j)
        return carry

    lax.fori_loop(0, (items + 1) >> 1, steps, 0)
    flush(items - 1)

    @pl.when(jnp.max(far[...]) > REACH * KAPPA * KAPPA)
    def _():
        def slow(i, carry):
            at = entry(i)
            columns = jnp.concatenate([src[at, 0:7], zero], axis=0).T
            y = [columns[:, a : a + 1] * KAPPA for a in range(3)]
            n = [columns[:, a + 3 : a + 4] * KAPPA for a in range(3)]
            position, lift, normal, tangent = circle(targ, at >> 4)
            center = position + lift
            tile[...] = jnp.zeros_like(tile)
            for m in range(CHECKS):
                point = center + math.cos(angle(m)) * normal + math.sin(angle(m)) * tangent
                for x in range(8):
                    rows = slice(16 * x, 16 * x + 16)
                    d = [point[a : a + 1] - y[a][rows] for a in range(3)]
                    square = d[0] * d[0] + d[1] * d[1] + d[2] * d[2]
                    facing = d[0] * n[0][rows] + d[1] * n[1][rows] + d[2] * n[2][rows]
                    tile[rows] += potential(square, facing, m)
            flush(i)
            return carry

        lax.fori_loop(0, items, slow, 0)


VMEM = pl.BlockSpec(memory_space=pltpu.VMEM)
KEPT = pl.BlockSpec(memory_space=pl.ANY)
WORK = [
    pltpu.VMEM((4, DEPTH, CHECKS * LANES), BF16),
    pltpu.VMEM((4, 8, LANES), F32),
    pltpu.VMEM((2, 2 * LANES, DEPTH), BF16),
    pltpu.VMEM((LANES, LANES), F32),
    pltpu.VMEM((2 * LANES, CHECKS * LANES), F32),
    pltpu.VMEM((8, LANES), F32),
]
SUMS = pltpu.VMEM((4, SLOTS * NODES, LANES), F32)


def cost(items):
    points = items * 128 * 128 * CHECKS
    return pl.CostEstimate(flops=40 * points, bytes_accessed=2 << 20, transcendentals=2 * points)


def coefficients_head(lists, lens, targ, ups, geom):
    return pl.pallas_call(
        head_body,
        grid_spec=pltpu.PrefetchScalarGridSpec(
            num_scalar_prefetch=2,
            grid=(1,),
            in_specs=[KEPT] * 3,
            out_specs=[VMEM] * 4 + [pl.BlockSpec(memory_space=pltpu.SMEM)],
            scratch_shapes=WORK + [pltpu.SemaphoreType.DMA((2,)), pltpu.SemaphoreType.DMA((4 * SLOTS,))],
        ),
        out_shape=[
            SUMS,
            pltpu.VMEM((4 * SLOTS, 8, LANES), F32),
            pltpu.VMEM(targ.shape, F32),
            pltpu.VMEM(ups.shape, F32),
            jax.ShapeDtypeStruct((4 * SLOTS + 1,), jnp.int32),
        ],
        cost_estimate=cost(60 - TAIL),
        compiler_params=pltpu.CompilerParams(vmem_limit_bytes=VMEM_ALL - 3800000),
        name="coefficients_head",
    )(lists, lens, targ, ups, geom)


def coefficients_tail(table, src, targ, ups):
    return pl.pallas_call(
        tail_body,
        grid_spec=pltpu.PrefetchScalarGridSpec(
            num_scalar_prefetch=1, grid=(1,), in_specs=[VMEM] * 3, out_specs=VMEM, scratch_shapes=WORK
        ),
        out_shape=SUMS,
        cost_estimate=cost(TAIL),
        compiler_params=pltpu.CompilerParams(vmem_limit_bytes=VMEM_KEPT),
        name="coefficients_tail",
    )(table, src, targ, ups)


def combine_body(lists, head, tail, own, across, beside, out, kept, sem):
    side = 1 - 2 * (lax.axis_index("patch") & 1)

    def nodes(e):
        which = ((e - 64) >> 8) * side
        edge = jnp.where(which < 0, across[e & 63], beside[e & 63])
        panel = (e - 64) & 255
        owner = panel >> 5
        owner = jnp.where(owner >= 4, 4 + ((owner - 1) & 3), owner)
        return jnp.where(which == 0, own[32 * owner + (panel & 31)], edge)

    stores = []
    for b in range(4):
        high, low = halves(jnp.concatenate([nodes(lists[b, l]) for l in range(SLOTS)], axis=0))
        c_high, c_low = halves((head[b] + tail[b]).T)
        value = jnp.dot(c_high, high, preferred_element_type=F32)
        value += jnp.dot(c_high, low, preferred_element_type=F32)
        value += jnp.dot(c_low, high, preferred_element_type=F32)
        kept[b] = value
        stores.append(pltpu.make_async_copy(kept.at[b], out.at[pl.ds(b * LANES, LANES)], sem.at[b]))
        stores[b].start()
    for store in stores:
        store.wait()


def combine(lists, head, tail, own, across, beside):
    return pl.pallas_call(
        combine_body,
        grid_spec=pltpu.PrefetchScalarGridSpec(
            num_scalar_prefetch=1,
            grid=(1,),
            in_specs=[VMEM] * 5,
            out_specs=KEPT,
            scratch_shapes=[pltpu.VMEM((4, LANES, LANES), F32), pltpu.SemaphoreType.DMA((4,))],
        ),
        out_shape=jax.ShapeDtypeStruct((4 * LANES, LANES), F32),
        cost_estimate=pl.CostEstimate(flops=4 << 24, bytes_accessed=4 << 20, transcendentals=0),
        compiler_params=pltpu.CompilerParams(vmem_limit_bytes=24 << 20),
        name="combine",
    )(lists, head, tail, own, across, beside)


def on_device(dens, upsample, src_geom, targ, lists, lens):
    groups = lax.axis_size("patch")
    geom = jnp.transpose(src_geom, (1, 0, 2))
    gathered = lax.all_to_all(spread(dens), "helper", 0, 0, axis_index_groups=[ORDER], tiled=True).reshape(256, NODES, LANES)
    head, src, targ, ups, table = coefficients_head(lists, lens, targ, upsample.T, geom)
    gathered, head = lax.optimization_barrier((gathered, head))
    odd = lax.axis_index("patch").astype(jnp.int32) & 1
    far_edge = lax.dynamic_slice_in_dim(gathered, 160 * odd, 64)
    near_edge = lax.dynamic_slice_in_dim(gathered, 160 - 160 * odd, 64)
    across = lax.ppermute(far_edge, "patch", [(g, (g + 2 * (g % 2) - 1) % groups) for g in range(groups)])
    beside = lax.ppermute(near_edge, "patch", [(g, g ^ 1) for g in range(groups)])
    tail = coefficients_tail(table, src, targ, ups)
    return combine(lists, head, tail, gathered, across, beside)


def solution(mesh):
    in_specs = (
        P(("patch", "helper"), None, None),
        P(),
        P("patch", None, None),
        P(None, ("patch", "helper")),
        P(("patch", "helper"), None),
        P(("patch", "helper")),
    )
    out_specs = P(("patch", "helper"), None)
    return jax.shard_map(on_device, mesh=mesh, in_specs=in_specs, out_specs=out_specs, check_vma=False)
```
